512 devices in a mesh: tm: 128 (over y, z, x_hi), space: 4 (over x_lo, core).
Axes of the slice: x: 4 (x_hi: 2, x_lo: 2; x = x_hi * 2 + x_lo), y: 4, z: 16, core: 2. Of those that a mesh axis runs over, the one named last changes fastest.
Arguments:
- video: bfloat16 [512, 8, 64, 192], P('tm', 'space'), may hold values from -45 to 45
- gain: float32 [192], replicated, may hold values from 0.1 to 1.9
- kernel: bfloat16 [3, 3, 3, 192, 192], replicated, may hold values from -0.078125 to 0.078125
- cotangent: bfloat16 [512, 8, 64, 192], P('tm', 'space'), may hold values from -6 to 6
Outputs:
- video_grad: bfloat16 [512, 8, 64, 192], P('tm', 'space')
- kernel_grad: float32 [995328], P(('tm', 'space'))
- gain_grad: float32 [192], replicated
The draws below stay inside these ranges and needn't reach their ends.
All inputs are finite; a program needn't handle non-finite values.
Results may differ from the reference program's by a relative error of at most 0.004.
Values may be sent and summed in bfloat16 or wider, within the bound.
A program may use at most 64 MiB of HBM per device.

```python
import math
import jax
import jax.numpy as jnp
from jax import lax

C = 192
WIDTH = 64
FRAMES = 512
ROWS = 8
N_TM = 128
N_SPACE = 4


def draw_video(key, part):
    key_channel, key_position, key_values = jax.random.split(key, 3)
    channel_scale = jnp.exp(jax.random.uniform(key_channel, (C,), jnp.float32, 0.0, math.log(10.0)))
    position_scale = jnp.exp(jax.random.uniform(key_position, (FRAMES, ROWS, WIDTH, 1), jnp.float32, 0.0, math.log(3.0)))
    values = jnp.clip(jax.random.normal(key_values, (FRAMES, ROWS, WIDTH, C), jnp.float32), -6.0, 6.0)
    return (values * channel_scale * position_scale * 0.25).astype(jnp.bfloat16)


def shard_levels(own_key, extent, shards, low, high):
    loudness, own = 1.0, jax.random.fold_in(own_key, 6)
    for dim, shards_of in shards:
        draws = jnp.exp(jax.random.uniform(jax.random.fold_in(own, dim), (shards_of,), jnp.float32, low / len(shards), high / len(shards)))
        loudness = loudness * jnp.repeat(draws, extent[dim] // shards_of).reshape([-1 if axis == dim else 1 for axis in range(len(extent))])
    return loudness


def scatter_about(stream_key, shape, width, limit, cuts=(), kind=jnp.bfloat16):
    result = width * jax.random.normal(stream_key, shape, jnp.float32)
    if cuts:
        result = result * shard_levels(stream_key, shape, cuts, -0.22, 0.18)
    return jnp.clip(result, -limit, limit).astype(kind)


def setup_inputs(seed: int = 0) -> dict:
    key_of = jax.random.split(jax.random.key(seed), 5)
    return {
        "video": draw_video(jax.random.fold_in(key_of[4], 71), 0),
        "gain": jnp.clip(1.0 + 0.18 * jax.random.normal(key_of[1], (C,), jnp.float32), 0.1, 1.9),
        "kernel": scatter_about(key_of[2], (3, 3, 3, C, C), (27 * C) ** -0.5, 0.078125),
        "cotangent": scatter_about(key_of[3], (FRAMES, ROWS, WIDTH, C), 1.0, 6.0, ((0, 128), (1, 4))),
    }


def forward_norm(video, gain):
    as_float = video.astype(jnp.float32)
    inverse = lax.rsqrt(lax.optimization_barrier(jnp.mean(as_float * as_float, axis=-1, keepdims=True)) + 1e-06)
    normed = as_float * inverse * gain
    hidden = jax.nn.silu(normed).astype(jnp.bfloat16)
    return (as_float, inverse, normed, hidden)

def reference(video, gain, kernel, cotangent):
    frame_count, row_count, col_count, channels = video.shape
    as_float, inverse, normed, hidden = forward_norm(video, gain)
    hidden_pad = jnp.pad(hidden, ((2, 0), (1, 1), (1, 1), (0, 0))).astype(jnp.float32)
    cot_flat = cotangent.reshape(-1, channels).astype(jnp.float32)
    kernel_float = kernel.astype(jnp.float32)
    pad_grad = jnp.zeros((frame_count + 2, row_count + 2, col_count + 2, channels), jnp.float32)
    tap_grads = []
    for offset_t in range(3):
        for offset_r in range(3):
            for offset_c in range(3):
                window = hidden_pad[offset_t:offset_t + frame_count, offset_r:offset_r + row_count, offset_c:offset_c + col_count].reshape(-1, channels)
                tap_grads.append(lax.dot_general(window, cot_flat, (((0,), (0,)), ((), ())), precision=lax.Precision.HIGHEST, preferred_element_type=jnp.float32))
                product = lax.dot_general(cot_flat, kernel_float[offset_t, offset_r, offset_c], (((1,), (1,)), ((), ())), precision=lax.Precision.HIGHEST, preferred_element_type=jnp.float32)
                pad_grad = pad_grad.at[offset_t:offset_t + frame_count, offset_r:offset_r + row_count, offset_c:offset_c + col_count].add(product.reshape(frame_count, row_count, col_count, channels))
    devices = N_TM * N_SPACE
    kernel_grad = jnp.stack(tap_grads).reshape(-1) / devices
    hidden_grad = pad_grad[2:, 1:row_count + 1, 1:col_count + 1]
    gate_value = jax.nn.sigmoid(normed)
    normed_grad = hidden_grad * gate_value * (1.0 + normed * (1.0 - gate_value))
    gain_grad = lax.optimization_barrier(jnp.sum((normed_grad * as_float * inverse).reshape(-1, channels), axis=0)) / devices
    scaled = normed_grad * gain
    video_grad = inverse * scaled - as_float * inverse ** 3 * lax.optimization_barrier(jnp.mean(scaled * as_float, axis=-1, keepdims=True))
    return (video_grad.astype(jnp.bfloat16), kernel_grad, gain_grad)
```

```python
import jax
import jax.numpy as jnp
from jax import lax
from jax.experimental import pallas as pl
from jax.experimental.pallas import tpu as pltpu
from jax.sharding import PartitionSpec as P

F32 = jnp.float32
BF16 = jnp.bfloat16
C = 192
TAPS = 27
MESH = pl.DeviceIdType.MESH


def shifted(block, axis, distance):
    devices = range(lax.axis_size(axis))
    route = [(i - distance, i) for i in devices if i - distance in devices]
    return lax.ppermute(block, axis, route)


def compute_kernel(video, gain, kernel, cot, vgrad, packed, wins, hid_t, ksum, acc):
    frames, rows, cols, _ = video.shape
    pixels = frames * rows * cols
    col = lax.broadcasted_iota(jnp.int32, (cols, C), 0)

    def shift_row(index, carry):
        f, r = lax.div(index, rows + 2), lax.rem(index, rows + 2)
        plain = cot[f, r]
        wide = plain.astype(F32)
        wins[0, f, r] = jnp.where(col == cols - 1, 0.0, pltpu.roll(wide, cols - 1, 0)).astype(BF16)
        wins[1, f, r] = plain
        wins[2, f, r] = jnp.where(col == 0, 0.0, pltpu.roll(wide, 1, 0)).astype(BF16)
        return carry

    lax.fori_loop(0, (frames + 2) * (rows + 2), shift_row, 0)
    wide = video[...].reshape(pixels, C).astype(F32)
    inverse = lax.rsqrt(jnp.mean(wide * wide, axis=-1, keepdims=True) + 1e-6)
    normed = wide * inverse * gain[...]
    gate = 1.0 / (1.0 + jnp.exp(-normed))
    hid_t[...] = (normed * gate).astype(BF16).astype(F32).T.astype(BF16)

    def window(tap):
        a, b, d = tap // 9, tap // 3 % 3, tap % 3
        block = wins[d, 2 - a : 2 - a + frames, 2 - b : 2 - b + rows]
        return block.reshape(pixels, C)

    for tap in range(TAPS):
        win = window(tap)
        ksum[tap * C : (tap + 1) * C, :] = jnp.dot(hid_t[...], win, preferred_element_type=F32)
    for tap in range(TAPS):
        term = lax.dot_general(
            window(tap), kernel[tap], (((1,), (1,)), ((), ())), preferred_element_type=F32
        )
        if tap == 0:
            acc[...] = term
        else:
            acc[...] += term
    wide = video[...].reshape(pixels, C).astype(F32)
    inverse = lax.rsqrt(jnp.mean(wide * wide, axis=-1, keepdims=True) + 1e-6)
    normed = wide * inverse * gain[...]
    gate = 1.0 / (1.0 + jnp.exp(-normed))
    ngrad = acc[...] * gate * (1.0 + normed * (1.0 - gate))
    gain_sum = jnp.sum(ngrad * wide * inverse, axis=0, keepdims=True)
    scaled = ngrad * gain[...]
    mean = jnp.mean(scaled * wide, axis=-1, keepdims=True)
    result = inverse * scaled - wide * (inverse * inverse * inverse) * mean
    vgrad[...] = result.astype(BF16).reshape(video.shape)

    line = lax.broadcasted_iota(jnp.int32, (16, 64), 0)
    spare = jnp.where(
        line == 3,
        gain_sum[:, 0:64],
        jnp.where(line == 4, gain_sum[:, 64:128], jnp.where(line == 5, gain_sum[:, 128:192], 0.0)),
    )

    def pack(group, carry):
        y, zh = lax.div(group, 2), lax.rem(group, 2)
        for k in range(8):
            z = zh * 8 + k
            first = 81 * k // 8 * 8
            off = 81 * k - first
            block = ksum[pl.ds(pl.multiple_of(group * 648 + first, 8), 96 if off else 88), :]
            block = block[off : off + 81]
            low, high = block[:, :128], block[:, 128:]
            for m in range(5):
                packed[m % 2, m // 2, y, z] = low[16 * m : 16 * m + 16].astype(BF16)
            for m in (5, 6):
                r = 32 * (m - 5)
                pair = jnp.concatenate([high[r : r + 16], high[r + 16 : r + 32]], axis=1)
                packed[m % 2, m // 2, y, z] = pair.astype(BF16)
            last = block[80:81]
            right = jnp.where(
                line == 0,
                last[:, 0:64],
                jnp.where(line == 1, last[:, 64:128], jnp.where(line == 2, last[:, 128:192], spare)),
            )
            packed[1, 3, y, z] = jnp.concatenate([high[64:80], right], axis=1).astype(BF16)
        return carry

    lax.fori_loop(0, 8, pack, 0)


def compute(video, gain, kernel, cot):
    frames, rows, cols, _ = video.shape
    pixels = frames * rows * cols
    vmem = pl.BlockSpec(memory_space=pltpu.VMEM)
    return pl.pallas_call(
        compute_kernel,
        out_shape=(
            jax.ShapeDtypeStruct(video.shape, BF16),
            jax.ShapeDtypeStruct((2, 4, 4, 16, 16, 128), BF16),
        ),
        in_specs=[vmem] * 4,
        out_specs=(vmem, vmem),
        scratch_shapes=[
            pltpu.VMEM((3, frames + 2, rows + 2, cols, C), BF16),
            pltpu.VMEM((C, pixels), BF16),
            pltpu.VMEM((TAPS * C + 8, C), F32),
            pltpu.VMEM((pixels, C), F32),
        ],
        compiler_params=pltpu.CompilerParams(vmem_limit_bytes=60 << 20),
        name="local_grads",
    )(video, gain.reshape(1, C), kernel.reshape(TAPS, C, C), cot)


def reduce_kernel(
    packed, out, rc, sx, rx, sy, ry, sx2, rx2, sy2, ry2, s3, r3, s4, r4,
    c_send, c_recv, a_send, a_recv, b_send, b_recv, z_send, z_recv, g_send, g_recv,
):
    t, s = lax.axis_index("tm"), lax.axis_index("space")
    y, z, x = lax.div(t, 32), lax.rem(lax.div(t, 2), 16), lax.rem(t, 2) * 2 + lax.div(s, 2)
    core = lax.rem(s, 2)
    member = x * 2 + core

    def device(y, z, x, core):
        return ((y * 16 + z) * 2 + lax.div(x, 2), lax.rem(x, 2) * 2 + core)

    def turn(index, r, n):
        return lax.rem(index + r, n)

    peers = [device(y, z, lax.div(m, 2), lax.rem(m, 2)) for m in (turn(member, r, 8) for r in range(1, 8))]
    peers += [device(turn(y, r, 4), z, x, core) for r in range(1, 4)]
    peers += [device(y, turn(z, r, 16), x, core) for r in range(1, 16)]
    barrier = pltpu.get_barrier_semaphore()
    for peer in peers:
        pl.semaphore_signal(barrier, inc=1, device_id=peer, device_id_type=MESH)
    pl.semaphore_wait(barrier, len(peers))

    def send(src, dst, send_sem, recv_sem, target):
        copy = pltpu.make_async_remote_copy(
            src_ref=src, dst_ref=dst, send_sem=send_sem, recv_sem=recv_sem,
            device_id=target, device_id_type=MESH,
        )
        copy.start()
        return copy

    def total(*terms):
        result = terms[0].astype(F32)
        for term in terms[1:]:
            result += term.astype(F32)
        return result

    order = (1, 3, 2, 0)
    other = 1 - core
    partner = device(y, z, x, other)
    c_copies = {}
    for i, r in enumerate(order):
        for half in range(2):
            k = i * 2 + half
            if half == 0:
                xt = turn(x, r, 4)
                src, dst = packed.at[other, xt, :, 0:8], rc.at[xt, :, 0:8]
            else:
                yt = turn(y, r, 4)
                src, dst = packed.at[other, :, yt, 8:16], rc.at[:, yt, 8:16]
            c_copies[r, half] = send(src, dst, c_send.at[k], c_recv.at[k], partner)
    first = {}
    for r in order[:3]:
        xt, yt = turn(x, r, 4), turn(y, r, 4)
        c_copies[r, 0].wait_recv()
        sx[r - 1] = total(packed[core, xt, :, 0:8], rc[xt, :, 0:8]).astype(BF16)
        first[r, 0] = send(sx.at[r - 1], rx.at[r - 1], a_send.at[r - 1], a_recv.at[r - 1], device(y, z, xt, core))
        c_copies[r, 1].wait_recv()
        sy[r - 1] = total(packed[core, :, yt, 8:16], rc[:, yt, 8:16]).astype(BF16)
        first[r, 1] = send(sy.at[r - 1], ry.at[r - 1], a_send.at[r + 2], a_recv.at[r + 2], device(yt, z, x, core))
    c_copies[0, 0].wait_recv()
    c_copies[0, 1].wait_recv()
    for r in order[:3]:
        first[r, 0].wait_recv()
        first[r, 1].wait_recv()

    def part_x(yt):
        return total(packed[core, x, yt, 0:8], rc[x, yt, 0:8], rx[0, yt], rx[1, yt], rx[2, yt])

    def part_y(xt):
        return total(packed[core, xt, y, 8:16], rc[xt, y, 8:16], ry[0, xt], ry[1, xt], ry[2, xt])

    second = {}
    for r in order[:3]:
        xt, yt = turn(x, r, 4), turn(y, r, 4)
        sy2[r - 1] = part_x(yt).astype(BF16)
        second[r, 0] = send(sy2.at[r - 1], ry2.at[r - 1], b_send.at[r - 1], b_recv.at[r - 1], device(yt, z, x, core))
        sx2[r - 1] = part_y(xt).astype(BF16)
        second[r, 1] = send(sx2.at[r - 1], rx2.at[r - 1], b_send.at[r + 2], b_recv.at[r + 2], device(y, z, xt, core))
    own_x, own_y = part_x(y), part_y(x)
    for r in order[:3]:
        second[r, 0].wait_recv()
        second[r, 1].wait_recv()
    s3[0:8] = total(own_x, ry2[0], ry2[1], ry2[2]).astype(BF16)
    s3[8:16] = total(own_y, rx2[0], rx2[1], rx2[2]).astype(BF16)
    third = []
    for r in (8, 7, 9, 6, 10, 5, 11, 4, 12, 3, 13, 2, 14, 1, 15):
        zt = turn(z, r, 16)
        third.append(
            send(s3.at[zt], r3.at[r - 1], z_send.at[r - 1], z_recv.at[r - 1], device(y, zt, x, core))
        )
    for copy in third:
        copy.wait_recv()
    final = s3[z].astype(F32)
    for r in range(15):
        final += r3[r].astype(F32)
    final *= 1.0 / 512
    s4[...] = final
    fourth = []
    for r in range(1, 8):
        m = turn(member, r, 8)
        fourth.append(
            send(
                s4, r4.at[r - 1], g_send.at[r - 1], g_recv.at[r - 1],
                device(y, z, lax.div(m, 2), lax.rem(m, 2)),
            )
        )
    out[member] = final
    for r, copy in enumerate(fourth, 1):
        copy.wait_recv()
        out[lax.rem(member + 8 - r, 8)] = r4[r - 1]
    for group in (c_copies.values(), first.values(), second.values(), third, fourth):
        for copy in group:
            copy.wait_send()


def reduce_scatter(packed):
    vmem = pl.BlockSpec(memory_space=pltpu.VMEM)

    def buffer(*shape, dtype=BF16):
        return pltpu.VMEM(shape + (16, 128), dtype)

    def dma(count):
        return pltpu.SemaphoreType.DMA((count,))

    return pl.pallas_call(
        reduce_kernel,
        out_shape=jax.ShapeDtypeStruct((8, 16, 128), F32),
        in_specs=[vmem],
        out_specs=vmem,
        scratch_shapes=[
            buffer(4, 4, 16),
            buffer(3, 4, 8), buffer(3, 4, 8), buffer(3, 4, 8), buffer(3, 4, 8),
            buffer(3, 8), buffer(3, 8), buffer(3, 8), buffer(3, 8),
            buffer(16), buffer(15),
            buffer(dtype=F32), buffer(7, dtype=F32),
            dma(8), dma(8), dma(6), dma(6), dma(6), dma(6), dma(15), dma(15), dma(7), dma(7),
        ],
        compiler_params=pltpu.CompilerParams(
            collective_id=0, has_side_effects=True, vmem_limit_bytes=40 << 20
        ),
        name="reduce_scatter",
    )(packed)


def unpack(tiles):
    low = tiles[0:5].reshape(80, 128)
    pairs = tiles[5:7].reshape(2, 16, 2, 64).transpose(0, 2, 1, 3).reshape(64, 64)
    high = jnp.concatenate([pairs, tiles[7, :, :64]], axis=0)
    main = jnp.concatenate([low, high], axis=1).reshape(-1)
    return jnp.concatenate([main, tiles[7, 0:3, 64:].reshape(-1)]), tiles[7, 3:6, 64:].reshape(-1)


def on_device(video, gain, kernel, cotangent):
    later = shifted(cotangent[:2], "tm", -1)
    ext = jnp.concatenate([cotangent, later], axis=0)
    above = shifted(ext[:, -1:], "space", 1)
    below = shifted(ext[:, :1], "space", -1)
    ext = jnp.concatenate([above, ext, below], axis=1)
    video_grad, packed = compute(video, gain, kernel, ext)
    tiles = reduce_scatter(packed)
    rows, gain_grad = unpack(tiles)
    member = lax.rem(lax.axis_index("tm"), 2) * 4 + lax.axis_index("space")
    share = lax.dynamic_slice_in_dim(rows, member * 1944, 1944)
    return video_grad, share, gain_grad


def solution(mesh):
    in_specs = (P("tm", "space", None, None), P(), P(), P("tm", "space", None, None))
    out_specs = (P("tm", "space", None, None), P(("tm", "space")), P())
    return jax.shard_map(
        on_device, mesh=mesh, in_specs=in_specs, out_specs=out_specs, check_vma=False
    )
```

```python
import jax
import jax.numpy as jnp
from jax import lax
from jax.experimental import pallas as pl
from jax.experimental.pallas import tpu as pltpu
from jax.sharding import PartitionSpec as P

F32 = jnp.float32
BF16 = jnp.bfloat16
C = 192
TAPS = 27
MESH = pl.DeviceIdType.MESH


def fused_kernel(
    video, gain, kernel_hbm, cot, vgrad, out, gain_out,
    kernel, ext, wins, hid_t, ksum, acc, packed,
    rc, sx, rx, sy, ry, sx2, rx2, sy2, ry2, s3, r3, s4, r4, g1, q1, g2, q2, g3, q3,
    k_sem, h_send, h_recv, c_send, c_recv, x_send, x_recv, y_send, y_recv,
    b_send, b_recv, z_send, z_recv, g_send, g_recv,
    q1_send, q1_recv, q2_send, q2_recv, q3_send, q3_recv,
):
    frames, rows, cols, _ = video.shape
    pixels = frames * rows * cols
    t, s = lax.axis_index("tm"), lax.axis_index("space")
    n_t, n_s = lax.axis_size("tm"), lax.axis_size("space")
    y, z, x = lax.div(t, 32), lax.rem(lax.div(t, 2), 16), lax.rem(t, 2) * 2 + lax.div(s, 2)
    core = lax.rem(s, 2)
    member = x * 2 + core

    def device(y, z, x, core):
        return ((y * 16 + z) * 2 + lax.div(x, 2), lax.rem(x, 2) * 2 + core)

    def turn(index, r, n):
        return lax.rem(index + r, n)

    def mate(r):
        m = turn(member, r, 8)
        return device(y, z, lax.div(m, 2), lax.rem(m, 2))

    next_t, prev_t = turn(t, 1, n_t), turn(t, n_t - 1, n_t)
    up, down = turn(s, n_s - 1, n_s), turn(s, 1, n_s)
    peers = [mate(r) for r in range(1, 8)]
    peers += [device(turn(y, r, 4), z, x, core) for r in range(1, 4)]
    peers += [device(y, turn(z, r, 16), x, core) for r in range(1, 16)]
    peers += [(next_t, s), (next_t, up), (next_t, down), (t, up), (t, down)]
    barrier = pltpu.get_barrier_semaphore()
    for peer in peers:
        pl.semaphore_signal(barrier, inc=1, device_id=peer, device_id_type=MESH)
    weights = pltpu.make_async_copy(kernel_hbm, kernel, k_sem)
    weights.start()

    def send(src, dst, send_sem, recv_sem, target):
        copy = pltpu.make_async_remote_copy(
            src_ref=src, dst_ref=dst, send_sem=send_sem, recv_sem=recv_sem,
            device_id=target, device_id_type=MESH,
        )
        copy.start()
        return copy

    def total(*terms):
        result = terms[0].astype(F32)
        for term in terms[1:]:
            result += term.astype(F32)
        return result

    col = lax.broadcasted_iota(jnp.int32, (cols, C), 0)

    def put(f, r, plain):
        wide = plain.astype(F32)
        wins[0, f, r] = jnp.where(col == cols - 1, 0.0, pltpu.roll(wide, cols - 1, 0)).astype(BF16)
        wins[1, f, r] = wide.astype(BF16)
        wins[2, f, r] = jnp.where(col == 0, 0.0, pltpu.roll(wide, 1, 0)).astype(BF16)

    def own_row(index, carry):
        f, r = lax.div(index, rows), lax.rem(index, rows)
        put(f, r + 1, cot[f, r])
        return carry

    lax.fori_loop(0, frames * rows, own_row, 0)

    def norm():
        wide = video[...].reshape(pixels, C).astype(F32)
        inverse = lax.rsqrt(jnp.mean(wide * wide, axis=-1, keepdims=True) + 1e-6)
        normed = wide * inverse * gain[...]
        return wide, inverse, normed, 1.0 / (1.0 + jnp.exp(-normed))

    _, _, normed, gate = norm()
    hid_t[...] = (normed * gate).astype(BF16).astype(F32).T.astype(BF16)

    pl.semaphore_wait(barrier, len(peers))
    halo = [
        (cot.at[0:2], ext.at[4:6, 1:3], (prev_t, s)),
        (cot.at[0:2, rows - 1], ext.at[4:6, 0], (prev_t, down)),
        (cot.at[0:2, 0], ext.at[4:6, 3], (prev_t, up)),
        (cot.at[:, rows - 1], ext.at[0:4, 0], (t, down)),
        (cot.at[:, 0], ext.at[0:4, 3], (t, up)),
    ]
    halo = [send(a, b, h_send.at[i], h_recv.at[i], d) for i, (a, b, d) in enumerate(halo)]

    def window(tap):
        a, b, d = tap // 9, tap // 3 % 3, tap % 3
        block = wins[d, 2 - a : 2 - a + frames, 2 - b : 2 - b + rows]
        return block.reshape(pixels, C)

    def kernel_term(tap):
        ksum[tap * C : (tap + 1) * C, :] = jnp.dot(
            hid_t[...], window(tap), preferred_element_type=F32
        )

    def hidden_term(tap, first=False):
        term = lax.dot_general(
            window(tap), kernel[tap], (((1,), (1,)), ((), ())), preferred_element_type=F32
        )
        if first:
            acc[...] = term
        else:
            acc[...] += term

    local_taps = (21, 22, 23)
    for tap in local_taps:
        kernel_term(tap)
    for copy in halo:
        copy.wait_recv()

    def far_row(index, carry):
        f, r = lax.div(index, 2), lax.rem(index, 2) * 3
        gone = ((r == 0) & (s == 0)) | ((r == 3) & (s == n_s - 1)) | ((f >= 4) & (t == n_t - 1))
        put(f, r, jnp.where(gone, 0.0, ext[f, r].astype(F32)))
        return carry

    def late_row(index, carry):
        f, r = lax.div(index, 2) + 4, lax.rem(index, 2) + 1
        put(f, r, jnp.where(t == n_t - 1, 0.0, ext[f, r].astype(F32)))
        return carry

    lax.fori_loop(0, 12, far_row, 0)
    lax.fori_loop(0, 4, late_row, 0)

    line = lax.broadcasted_iota(jnp.int32, (16, 64), 0)

    def pack(quarter):
        def half(zh, carry):
            for k in range(8):
                where = zh * 8 + k
                first = 81 * k // 8 * 8
                off = 81 * k - first
                start = pl.multiple_of((quarter * 2 + zh) * 648 + first, 8)
                block = ksum[pl.ds(start, 96 if off else 88), :][off : off + 81]
                low, high = block[:, :128], block[:, 128:]
                for m in range(5):
                    packed[m % 2, m // 2, quarter, where] = low[16 * m : 16 * m + 16].astype(BF16)
                for m in (5, 6):
                    r = 32 * (m - 5)
                    pair = jnp.concatenate([high[r : r + 16], high[r + 16 : r + 32]], axis=1)
                    packed[m % 2, m // 2, quarter, where] = pair.astype(BF16)
                last = block[80:81]
                right = jnp.where(
                    line == 0,
                    last[:, 0:64],
                    jnp.where(line == 1, last[:, 64:128], jnp.where(line == 2, last[:, 128:192], 0.0)),
                )
                packed[1, 3, quarter, where] = jnp.concatenate([high[64:80], right], axis=1).astype(BF16)
            return carry

        lax.fori_loop(0, 2, half, 0)

    order = (1, 3, 2)
    other = 1 - core
    partner = device(y, z, x, other)
    pair_copies, x_copies, y_copies = {}, {}, {}

    def pair_stage(quarter):
        pair_copies[quarter].wait_recv()
        for r in order:
            xt = turn(x, r, 4)
            i = quarter * 3 + r - 1
            sx[r - 1, quarter] = total(packed[core, xt, quarter, 0:8], rc[quarter, xt, 0:8]).astype(BF16)
            x_copies[r, quarter] = send(
                sx.at[r - 1, quarter], rx.at[r - 1, quarter], x_send.at[i], x_recv.at[i], device(y, z, xt, core)
            )

    done = 0
    for quarter in range(4):
        until = (7, 14, 21, 27)[quarter]
        for tap in range(done, until):
            if tap not in local_taps:
                kernel_term(tap)
        done = until
        pack(quarter)
        pair_copies[quarter] = send(
            packed.at[other, :, quarter], rc.at[quarter], c_send.at[quarter], c_recv.at[quarter], partner
        )
        if quarter:
            pair_stage(quarter - 1)
    weights.wait()
    early = 4
    for tap in range(early):
        hidden_term(tap, tap == 0)
    pair_stage(3)
    for r in order:
        yt = turn(y, r, 4)
        sy[r - 1] = total(packed[core, :, yt, 8:16], rc[yt, :, 8:16]).astype(BF16)
        y_copies[r] = send(
            sy.at[r - 1], ry.at[r - 1], y_send.at[r - 1], y_recv.at[r - 1], device(turn(y, r, 4), z, x, core)
        )
    for tap in range(early, TAPS):
        hidden_term(tap)
    wide, inverse, normed, gate = norm()
    ngrad = acc[...] * gate * (1.0 + normed * (1.0 - gate))
    gain_sum = jnp.sum(ngrad * wide * inverse, axis=0, keepdims=True)
    g1[0:1, :] = gain_sum[:, :128]
    g1[1:2, :] = jnp.concatenate([gain_sum[:, 128:], jnp.zeros((1, 64), F32)], axis=1)
    gain_copies = [
        send(g1, q1.at[r - 1], q1_send.at[r - 1], q1_recv.at[r - 1], mate(r)) for r in range(1, 8)
    ]
    scaled = ngrad * gain[...]
    mean = jnp.mean(scaled * wide, axis=-1, keepdims=True)
    result = inverse * scaled - wide * (inverse * inverse * inverse) * mean
    vgrad[...] = result.astype(BF16).reshape(video.shape)

    for copy in x_copies.values():
        copy.wait_recv()
    for copy in y_copies.values():
        copy.wait_recv()

    def part_x(yt):
        return total(packed[core, x, yt, 0:8], rc[yt, x, 0:8], rx[0, yt], rx[1, yt], rx[2, yt])

    def part_y(xt):
        return total(packed[core, xt, y, 8:16], rc[y, xt, 8:16], ry[0, xt], ry[1, xt], ry[2, xt])

    second = {}
    for r in order:
        xt, yt = turn(x, r, 4), turn(y, r, 4)
        sy2[r - 1] = part_x(yt).astype(BF16)
        second[r, 0] = send(
            sy2.at[r - 1], ry2.at[r - 1], b_send.at[r - 1], b_recv.at[r - 1], device(yt, z, x, core)
        )
        sx2[r - 1] = part_y(xt).astype(BF16)
        second[r, 1] = send(
            sx2.at[r - 1], rx2.at[r - 1], b_send.at[r + 2], b_recv.at[r + 2], device(y, z, xt, core)
        )
    for copy in gain_copies:
        copy.wait_recv()
    g2[...] = total(g1[...], *(q1[r] for r in range(7)))
    gain_second = [
        send(g2, q2.at[r - 1], q2_send.at[r - 1], q2_recv.at[r - 1], device(turn(y, r, 4), z, x, core))
        for r in range(1, 4)
    ]
    own_x, own_y = part_x(y), part_y(x)
    for copy in second.values():
        copy.wait_recv()
    s3[0:8] = total(own_x, ry2[0], ry2[1], ry2[2]).astype(BF16)
    s3[8:16] = total(own_y, rx2[0], rx2[1], rx2[2]).astype(BF16)
    third, gain_third = [], []
    hops = (8, 7, 9, 6, 10, 5, 11, 4, 12, 3, 13, 2, 14, 1, 15)
    for r in hops:
        zt = turn(z, r, 16)
        third.append(
            send(s3.at[zt], r3.at[r - 1], z_send.at[r - 1], z_recv.at[r - 1], device(y, zt, x, core))
        )
    for copy in gain_second:
        copy.wait_recv()
    g3[...] = total(g2[...], *(q2[r] for r in range(3)))
    for r in hops:
        gain_third.append(
            send(g3, q3.at[r - 1], q3_send.at[r - 1], q3_recv.at[r - 1], device(y, turn(z, r, 16), x, core))
        )
    for copy in third:
        copy.wait_recv()
    final = total(s3[z], *(r3[r] for r in range(15))) * (1.0 / 512)
    s4[...] = final
    fourth = [
        send(s4, r4.at[r - 1], g_send.at[r - 1], g_recv.at[r - 1], mate(r)) for r in range(1, 8)
    ]
    out[member] = final
    for copy in gain_third:
        copy.wait_recv()
    gain_out[...] = total(g3[...], *(q3[r] for r in range(15))) * (1.0 / 512)
    for r, copy in enumerate(fourth, 1):
        copy.wait_recv()
        out[lax.rem(member + 8 - r, 8)] = r4[r - 1]
    for group in (
        halo, pair_copies.values(), x_copies.values(), y_copies.values(), gain_copies,
        second.values(), gain_second, third, gain_third, fourth,
    ):
        for copy in group:
            copy.wait_send()


def fused(video, gain, kernel, cot):
    frames, rows, cols, _ = video.shape
    pixels = frames * rows * cols
    vmem = pl.BlockSpec(memory_space=pltpu.VMEM)

    def tiles(*shape, dtype=BF16):
        return pltpu.VMEM(shape + (16, 128), dtype)

    def line(*shape):
        return pltpu.VMEM(shape + (2, 128), F32)

    def dma(count):
        return [pltpu.SemaphoreType.DMA((count,))] * 2

    return pl.pallas_call(
        fused_kernel,
        out_shape=(
            jax.ShapeDtypeStruct(video.shape, BF16),
            jax.ShapeDtypeStruct((8, 16, 128), F32),
            jax.ShapeDtypeStruct((2, 128), F32),
        ),
        in_specs=[vmem, vmem, pl.BlockSpec(memory_space=pl.ANY), vmem],
        out_specs=(vmem, vmem, vmem),
        scratch_shapes=[
            pltpu.VMEM((TAPS, C, C), BF16),
            pltpu.VMEM((frames + 2, rows + 2, cols, C), BF16),
            pltpu.VMEM((3, frames + 2, rows + 2, cols, C), BF16),
            pltpu.VMEM((C, pixels), BF16),
            pltpu.VMEM((TAPS * C + 8, C), F32),
            pltpu.VMEM((pixels, C), F32),
            tiles(2, 4, 4, 16),
            tiles(4, 4, 16),
            tiles(3, 4, 8), tiles(3, 4, 8), tiles(3, 4, 8), tiles(3, 4, 8),
            tiles(3, 8), tiles(3, 8), tiles(3, 8), tiles(3, 8),
            tiles(16), tiles(15),
            tiles(dtype=F32), tiles(7, dtype=F32),
            line(), line(7), line(), line(3), line(), line(15),
            pltpu.SemaphoreType.DMA,
            *dma(5), *dma(4), *dma(12), *dma(3), *dma(6), *dma(15), *dma(7),
            *dma(7), *dma(3), *dma(15),
        ],
        compiler_params=pltpu.CompilerParams(
            collective_id=0, has_side_effects=True, vmem_limit_bytes=60 << 20
        ),
        name="fused_backward",
    )(video, gain.reshape(1, C), kernel.reshape(TAPS, C, C), cot)


def unpack(tiles):
    low = tiles[0:5].reshape(80, 128)
    pairs = tiles[5:7].reshape(2, 16, 2, 64).transpose(0, 2, 1, 3).reshape(64, 64)
    high = jnp.concatenate([pairs, tiles[7, :, :64]], axis=0)
    main = jnp.concatenate([low, high], axis=1).reshape(-1)
    return jnp.concatenate([main, tiles[7, 0:3, 64:].reshape(-1)])


def on_device(video, gain, kernel, cotangent):
    video_grad, tiles, gain_rows = fused(video, gain, kernel, cotangent)
    member = lax.rem(lax.axis_index("tm"), 2) * 4 + lax.axis_index("space")
    share = lax.dynamic_slice_in_dim(unpack(tiles), member * 1944, 1944)
    return video_grad, share, gain_rows.reshape(-1)[:C]


def solution(mesh):
    in_specs = (P("tm", "space", None, None), P(), P(), P("tm", "space", None, None))
    out_specs = (P("tm", "space", None, None), P(("tm", "space")), P())
    return jax.shard_map(
        on_device, mesh=mesh, in_specs=in_specs, out_specs=out_specs, check_vma=False
    )
```

```python
import jax
import jax.numpy as jnp
from jax import lax
from jax.experimental import pallas as pl
from jax.experimental.pallas import tpu as pltpu
from jax.sharding import PartitionSpec as P

F32 = jnp.float32
BF16 = jnp.bfloat16
C = 192
TAPS = 27
MESH = pl.DeviceIdType.MESH
XZ = 10
NEAR = 4


def fused_kernel(
    video, gain, kernel_hbm, cot, vgrad, out, gain_out,
    kernel, ext, wins, hid_t, ksum, acc, packed,
    rc, sx, rx, sy, ry, sx2, rx2, sy2, ry2, s3, r3, s4, r4, g1, q1, g2, q2, g3, q3,
    k_sem, far_sem, h_send, h_recv, c_send, c_recv, x_send, x_recv, y_send, y_recv,
    b_send, b_recv, z_send, z_recv, g_send, g_recv,
    q1_send, q1_recv, q2_send, q2_recv, q3_send, q3_recv,
):
    frames, rows, cols, _ = video.shape
    pixels = frames * rows * cols
    t, s = lax.axis_index("tm"), lax.axis_index("space")
    n_t, n_s = lax.axis_size("tm"), lax.axis_size("space")
    y, z, x = lax.div(t, 32), lax.rem(lax.div(t, 2), 16), lax.rem(t, 2) * 2 + lax.div(s, 2)
    core = lax.rem(s, 2)
    member = x * 2 + core

    def device(y, z, x, core):
        return ((y * 16 + z) * 2 + lax.div(x, 2), lax.rem(x, 2) * 2 + core)

    def turn(index, r, n):
        return lax.rem(index + r, n)

    def mate(r):
        m = turn(member, r, 8)
        return device(y, z, lax.div(m, 2), lax.rem(m, 2))

    next_t, prev_t = turn(t, 1, n_t), turn(t, n_t - 1, n_t)
    up, down = turn(s, n_s - 1, n_s), turn(s, 1, n_s)
    peers = [mate(r) for r in range(1, 8)]
    peers += [device(turn(y, r, 4), z, x, core) for r in range(1, 4)]
    peers += [device(y, turn(z, r, 16), x, core) for r in range(1, 16) if min(r, 16 - r) <= NEAR]
    peers += [(next_t, s), (next_t, up), (next_t, down), (t, up), (t, down)]
    barrier = pltpu.get_barrier_semaphore()
    for peer in peers:
        pl.semaphore_signal(barrier, inc=1, device_id=peer, device_id_type=MESH)
    weights = pltpu.make_async_copy(kernel_hbm, kernel, k_sem)
    weights.start()

    def send(src, dst, send_sem, recv_sem, target):
        copy = pltpu.make_async_remote_copy(
            src_ref=src, dst_ref=dst, send_sem=send_sem, recv_sem=recv_sem,
            device_id=target, device_id_type=MESH,
        )
        copy.start()
        return copy

    def total(*terms):
        result = terms[0].astype(F32)
        for term in terms[1:]:
            result += term.astype(F32)
        return result

    col = lax.broadcasted_iota(jnp.int32, (cols, C), 0)

    def put(f, r, plain):
        wide = plain.astype(F32)
        wins[0, f, r] = jnp.where(col == cols - 1, 0.0, pltpu.roll(wide, cols - 1, 0)).astype(BF16)
        wins[1, f, r] = wide.astype(BF16)
        wins[2, f, r] = jnp.where(col == 0, 0.0, pltpu.roll(wide, 1, 0)).astype(BF16)

    def own_row(index, carry):
        f, r = lax.div(index, rows), lax.rem(index, rows)
        put(f, r + 1, cot[f, r])
        return carry

    lax.fori_loop(0, frames * rows, own_row, 0)

    def norm():
        wide = video[...].reshape(pixels, C).astype(F32)
        inverse = lax.rsqrt(jnp.mean(wide * wide, axis=-1, keepdims=True) + 1e-6)
        normed = wide * inverse * gain[...]
        return wide, inverse, normed, 1.0 / (1.0 + jnp.exp(-normed))

    _, _, normed, gate = norm()
    hid_t[...] = (normed * gate).astype(BF16).astype(F32).T.astype(BF16)

    pl.semaphore_wait(barrier, len(peers))
    for r in (NEAR, 16 - NEAR):
        pl.semaphore_signal(
            far_sem, inc=1, device_id=device(y, turn(z, r, 16), x, core), device_id_type=MESH
        )
    halo = [
        (cot.at[0:2], ext.at[4:6, 1:3], (prev_t, s)),
        (cot.at[0:2, rows - 1], ext.at[4:6, 0], (prev_t, down)),
        (cot.at[0:2, 0], ext.at[4:6, 3], (prev_t, up)),
        (cot.at[:, rows - 1], ext.at[0:4, 0], (t, down)),
        (cot.at[:, 0], ext.at[0:4, 3], (t, up)),
    ]
    halo = [send(a, b, h_send.at[i], h_recv.at[i], d) for i, (a, b, d) in enumerate(halo)]

    def window(tap):
        a, b, d = tap // 9, tap // 3 % 3, tap % 3
        block = wins[d, 2 - a : 2 - a + frames, 2 - b : 2 - b + rows]
        return block.reshape(pixels, C)

    def kernel_term(tap):
        ksum[tap * C : (tap + 1) * C, :] = jnp.dot(
            hid_t[...], window(tap), preferred_element_type=F32
        )

    def hidden_term(tap, first=False):
        term = lax.dot_general(
            window(tap), kernel[tap], (((1,), (1,)), ((), ())), preferred_element_type=F32
        )
        if first:
            acc[...] = term
        else:
            acc[...] += term

    local_taps = (21, 22, 23)
    for tap in local_taps:
        kernel_term(tap)
    for copy in halo:
        copy.wait_recv()

    def far_row(index, carry):
        f, r = lax.div(index, 2), lax.rem(index, 2) * 3
        gone = ((r == 0) & (s == 0)) | ((r == 3) & (s == n_s - 1)) | ((f >= 4) & (t == n_t - 1))
        put(f, r, jnp.where(gone, 0.0, ext[f, r].astype(F32)))
        return carry

    def late_row(index, carry):
        f, r = lax.div(index, 2) + 4, lax.rem(index, 2) + 1
        put(f, r, jnp.where(t == n_t - 1, 0.0, ext[f, r].astype(F32)))
        return carry

    lax.fori_loop(0, 12, far_row, 0)
    lax.fori_loop(0, 4, late_row, 0)

    line = lax.broadcasted_iota(jnp.int32, (16, 64), 0)

    def pack(quarter):
        for where in range(16):
            row = (quarter * 16 + where) * 81
            block = ksum[row : row + 81, :]
            low, high = block[:, :128], block[:, 128:]
            for m in range(5):
                packed[m % 2, m // 2, quarter, where] = low[16 * m : 16 * m + 16].astype(BF16)
            for m in (5, 6):
                r = 32 * (m - 5)
                pair = jnp.concatenate([high[r : r + 16], high[r + 16 : r + 32]], axis=1)
                packed[m % 2, m // 2, quarter, where] = pair.astype(BF16)
            last = block[80:81]
            right = jnp.where(
                line == 0,
                last[:, 0:64],
                jnp.where(line == 1, last[:, 64:128], jnp.where(line == 2, last[:, 128:192], 0.0)),
            )
            packed[1, 3, quarter, where] = jnp.concatenate([high[64:80], right], axis=1).astype(BF16)

    order = (1, 3, 2)
    other = 1 - core
    partner = device(y, z, x, other)
    pair_copies, x_copies, y_copies = {}, {}, {}

    def pair_stage(quarter):
        pair_copies[quarter].wait_recv()
        for r in order:
            xt = turn(x, r, 4)
            i = quarter * 3 + r - 1
            sx[r - 1, quarter] = total(packed[core, xt, quarter, 0:XZ], rc[quarter, xt, 0:XZ]).astype(BF16)
            x_copies[r, quarter] = send(
                sx.at[r - 1, quarter], rx.at[r - 1, quarter], x_send.at[i], x_recv.at[i], device(y, z, xt, core)
            )

    done = 0
    for quarter in range(4):
        until = (7, 14, 21, 27)[quarter]
        for tap in range(done, until):
            if tap not in local_taps:
                kernel_term(tap)
        done = until
        pack(quarter)
        pair_copies[quarter] = send(
            packed.at[other, :, quarter], rc.at[quarter], c_send.at[quarter], c_recv.at[quarter], partner
        )
        if quarter:
            pair_stage(quarter - 1)
    weights.wait()
    early = 4
    for tap in range(early):
        hidden_term(tap, tap == 0)
    pair_stage(3)
    for r in order:
        yt = turn(y, r, 4)
        sy[r - 1] = total(packed[core, :, yt, XZ:16], rc[yt, :, XZ:16]).astype(BF16)
        y_copies[r] = send(
            sy.at[r - 1], ry.at[r - 1], y_send.at[r - 1], y_recv.at[r - 1], device(turn(y, r, 4), z, x, core)
        )
    for tap in range(early, TAPS):
        hidden_term(tap)
    wide, inverse, normed, gate = norm()
    ngrad = acc[...] * gate * (1.0 + normed * (1.0 - gate))
    gain_sum = jnp.sum(ngrad * wide * inverse, axis=0, keepdims=True)
    g1[0:1, :] = gain_sum[:, :128]
    g1[1:2, :] = jnp.concatenate([gain_sum[:, 128:], jnp.zeros((1, 64), F32)], axis=1)
    gain_copies = [
        send(g1, q1.at[r - 1], q1_send.at[r - 1], q1_recv.at[r - 1], mate(r)) for r in range(1, 8)
    ]
    scaled = ngrad * gain[...]
    mean = jnp.mean(scaled * wide, axis=-1, keepdims=True)
    result = inverse * scaled - wide * (inverse * inverse * inverse) * mean
    vgrad[...] = result.astype(BF16).reshape(video.shape)

    for copy in x_copies.values():
        copy.wait_recv()
    for copy in y_copies.values():
        copy.wait_recv()

    def part_x(yt):
        return total(packed[core, x, yt, 0:XZ], rc[yt, x, 0:XZ], rx[0, yt], rx[1, yt], rx[2, yt])

    def part_y(xt):
        return total(packed[core, xt, y, XZ:16], rc[y, xt, XZ:16], ry[0, xt], ry[1, xt], ry[2, xt])

    second = {}
    for r in order:
        xt, yt = turn(x, r, 4), turn(y, r, 4)
        sy2[r - 1] = part_x(yt).astype(BF16)
        second[r, 0] = send(
            sy2.at[r - 1], ry2.at[r - 1], b_send.at[r - 1], b_recv.at[r - 1], device(yt, z, x, core)
        )
        sx2[r - 1] = part_y(xt).astype(BF16)
        second[r, 1] = send(
            sx2.at[r - 1], rx2.at[r - 1], b_send.at[r + 2], b_recv.at[r + 2], device(y, z, xt, core)
        )
    for copy in gain_copies:
        copy.wait_recv()
    g2[...] = total(g1[...], *(q1[r] for r in range(7)))
    gain_second = [
        send(g2, q2.at[r - 1], q2_send.at[r - 1], q2_recv.at[r - 1], device(turn(y, r, 4), z, x, core))
        for r in range(1, 4)
    ]
    own_x, own_y = part_x(y), part_y(x)
    for copy in second.values():
        copy.wait_recv()
    s3[0:XZ] = total(own_x, ry2[0], ry2[1], ry2[2]).astype(BF16)
    s3[XZ:16] = total(own_y, rx2[0], rx2[1], rx2[2]).astype(BF16)
    pl.semaphore_wait(far_sem, 2)
    third, gain_third = [], []
    hops = (8, 7, 9, 6, 10, 5, 11, 4, 12, 3, 13, 2, 14, 1, 15)
    for r in hops:
        zt = turn(z, r, 16)
        third.append(
            send(s3.at[zt], r3.at[r - 1], z_send.at[r - 1], z_recv.at[r - 1], device(y, zt, x, core))
        )
    for copy in gain_second:
        copy.wait_recv()
    g3[...] = total(g2[...], *(q2[r] for r in range(3)))
    for r in hops:
        gain_third.append(
            send(g3, q3.at[r - 1], q3_send.at[r - 1], q3_recv.at[r - 1], device(y, turn(z, r, 16), x, core))
        )
    for copy in third:
        copy.wait_recv()
    final = total(s3[z], *(r3[r] for r in range(15))) * (1.0 / 512)
    s4[...] = final
    fourth = [
        send(s4, r4.at[r - 1], g_send.at[r - 1], g_recv.at[r - 1], mate(r)) for r in range(1, 8)
    ]
    out[member] = final
    for copy in gain_third:
        copy.wait_recv()
    gain_out[...] = total(g3[...], *(q3[r] for r in range(15))) * (1.0 / 512)
    for r, copy in enumerate(fourth, 1):
        copy.wait_recv()
        out[lax.rem(member + 8 - r, 8)] = r4[r - 1]
    for group in (
        halo, pair_copies.values(), x_copies.values(), y_copies.values(), gain_copies,
        second.values(), gain_second, third, gain_third, fourth,
    ):
        for copy in group:
            copy.wait_send()


def fused(video, gain, kernel, cot):
    frames, rows, cols, _ = video.shape
    pixels = frames * rows * cols
    vmem = pl.BlockSpec(memory_space=pltpu.VMEM)

    def tiles(*shape, dtype=BF16):
        return pltpu.VMEM(shape + (16, 128), dtype)

    def line(*shape):
        return pltpu.VMEM(shape + (2, 128), F32)

    def dma(count):
        return [pltpu.SemaphoreType.DMA((count,))] * 2

    return pl.pallas_call(
        fused_kernel,
        out_shape=(
            jax.ShapeDtypeStruct(video.shape, BF16),
            jax.ShapeDtypeStruct((8, 16, 128), F32),
            jax.ShapeDtypeStruct((2, 128), F32),
        ),
        in_specs=[vmem, vmem, pl.BlockSpec(memory_space=pl.ANY), vmem],
        out_specs=(vmem, vmem, vmem),
        scratch_shapes=[
            pltpu.VMEM((TAPS, C, C), BF16),
            pltpu.VMEM((frames + 2, rows + 2, cols, C), BF16),
            pltpu.VMEM((3, frames + 2, rows + 2, cols, C), BF16),
            pltpu.VMEM((C, pixels), BF16),
            pltpu.VMEM((TAPS * C, C), F32),
            pltpu.VMEM((pixels, C), F32),
            tiles(2, 4, 4, 16),
            tiles(4, 4, 16),
            tiles(3, 4, XZ), tiles(3, 4, XZ), tiles(3, 4, 16 - XZ), tiles(3, 4, 16 - XZ),
            tiles(3, 16 - XZ), tiles(3, 16 - XZ), tiles(3, XZ), tiles(3, XZ),
            tiles(16), tiles(15),
            tiles(dtype=F32), tiles(7, dtype=F32),
            line(), line(7), line(), line(3), line(), line(15),
            pltpu.SemaphoreType.DMA, pltpu.SemaphoreType.REGULAR,
            *dma(5), *dma(4), *dma(12), *dma(3), *dma(6), *dma(15), *dma(7),
            *dma(7), *dma(3), *dma(15),
        ],
        compiler_params=pltpu.CompilerParams(
            collective_id=0, has_side_effects=True, vmem_limit_bytes=59 << 20
        ),
        name="fused_backward",
    )(video, gain.reshape(1, C), kernel.reshape(TAPS, C, C), cot)


def finish_kernel(vgrad, tiles, gain_rows, vgrad_out, share, gain_out, low, high, lines):
    t, s = lax.axis_index("tm"), lax.axis_index("space")
    member = lax.rem(t, 2) * 4 + s
    vgrad_out[...] = vgrad[...]
    gain_out[0:128] = gain_rows[0]
    gain_out[128:C] = gain_rows[1, : C - 128]
    for m in range(5):
        low[16 * m : 16 * m + 16, :] = tiles[m]
    for m in (5, 6):
        r = 32 * (m - 5)
        high[r : r + 16, 0:64] = tiles[m, :, 0:64]
        high[r + 16 : r + 32, 0:64] = tiles[m, :, 64:128]
    high[64:80, 0:64] = tiles[7, :, 0:64]
    low[80:81, :] = jnp.concatenate([tiles[7, 0:1, 64:], tiles[7, 1:2, 64:]], axis=1)
    high[80:81, 0:64] = tiles[7, 2:3, 64:]
    even_low, odd_low = low[pl.ds(0, 41, stride=2), :], low[pl.ds(1, 40, stride=2), :]
    even_high, odd_high = high[pl.ds(0, 41, stride=2), :], high[pl.ds(1, 40, stride=2), :]
    lines[pl.ds(0, 41, stride=3), :] = even_low
    lines[pl.ds(1, 40, stride=3), :] = jnp.concatenate([even_high[:40, :64], odd_low[:, :64]], axis=1)
    lines[pl.ds(2, 40, stride=3), :] = jnp.concatenate([odd_low[:, 64:], odd_high[:, :64]], axis=1)
    lines[121:122, :] = even_high[40:41]
    start, turned = 15 * member + lax.div(24 * member, 128), lax.rem(24 * member, 128)
    back = lax.rem(128 - turned, 128)
    lane = lax.broadcasted_iota(jnp.int32, (16, 128), 1)
    result = jnp.where(
        lane + turned < 128,
        pltpu.roll(lines[pl.ds(start, 16), :], back, 1),
        pltpu.roll(lines[pl.ds(start + 1, 16), :], back, 1),
    )
    for a in range(15):
        share[128 * a : 128 * a + 128] = result[a]
    share[1920:1944] = result[15, :24]


def finish(vgrad, tiles, gain_rows):
    vmem = pl.BlockSpec(memory_space=pltpu.VMEM)
    return pl.pallas_call(
        finish_kernel,
        out_shape=(
            jax.ShapeDtypeStruct(vgrad.shape, BF16),
            jax.ShapeDtypeStruct((1944,), F32),
            jax.ShapeDtypeStruct((C,), F32),
        ),
        in_specs=[vmem] * 3,
        out_specs=(vmem,) * 3,
        scratch_shapes=[
            pltpu.VMEM((88, 128), F32), pltpu.VMEM((88, 128), F32), pltpu.VMEM((144, 128), F32),
        ],
        compiler_params=pltpu.CompilerParams(vmem_limit_bytes=8 << 20),
        name="finish",
    )(vgrad, tiles, gain_rows)


def on_device(video, gain, kernel, cotangent):
    return finish(*fused(video, gain, kernel, cotangent))


def solution(mesh):
    in_specs = (P("tm", "space", None, None), P(), P(), P("tm", "space", None, None))
    out_specs = (P("tm", "space", None, None), P(("tm", "space")), P())
    return jax.shard_map(
        on_device, mesh=mesh, in_specs=in_specs, out_specs=out_specs, check_vma=False
    )
```

```python
import jax
import jax.numpy as jnp
from jax import lax
from jax.experimental import pallas as pl
from jax.experimental.pallas import tpu as pltpu
from jax.sharding import PartitionSpec as P

F32 = jnp.float32
BF16 = jnp.bfloat16
C = 192
TAPS = 27
MESH = pl.DeviceIdType.MESH
XZ = 10
NEAR = 4


def fused_kernel(
    video, gain, kernel_hbm, cot, vgrad, out, gain_out,
    kernel, ext, wins, hid_t, klow, khigh, lines, acc, packed,
    rc, sx, rx, sy, ry, sx2, rx2, sy2, ry2, s3, r3, g1, q1, g2, q2, g3, q3,
    k_sem, far_sem, h_send, h_recv, c_send, c_recv, x_send, x_recv, y_send, y_recv,
    b_send, b_recv, z_send, z_recv,
    q1_send, q1_recv, q2_send, q2_recv, q3_send, q3_recv,
):
    frames, rows, cols, _ = video.shape
    pixels = frames * rows * cols
    t, s = lax.axis_index("tm"), lax.axis_index("space")
    n_t, n_s = lax.axis_size("tm"), lax.axis_size("space")
    y, z, x = lax.div(t, 32), lax.rem(lax.div(t, 2), 16), lax.rem(t, 2) * 2 + lax.div(s, 2)
    core = lax.rem(s, 2)
    member = x * 2 + core

    def device(y, z, x, core):
        return ((y * 16 + z) * 2 + lax.div(x, 2), lax.rem(x, 2) * 2 + core)

    def turn(index, r, n):
        return lax.rem(index + r, n)

    def mate(r):
        m = turn(member, r, 8)
        return device(y, z, lax.div(m, 2), lax.rem(m, 2))

    next_t, prev_t = turn(t, 1, n_t), turn(t, n_t - 1, n_t)
    up, down = turn(s, n_s - 1, n_s), turn(s, 1, n_s)
    peers = [mate(r) for r in range(1, 8)]
    peers += [device(turn(y, r, 4), z, x, core) for r in range(1, 4)]
    peers += [device(y, turn(z, r, 16), x, core) for r in range(1, 16) if min(r, 16 - r) <= NEAR]
    peers += [(next_t, s), (next_t, up), (next_t, down), (t, up), (t, down)]
    barrier = pltpu.get_barrier_semaphore()
    for peer in peers:
        pl.semaphore_signal(barrier, inc=1, device_id=peer, device_id_type=MESH)
    weights = pltpu.make_async_copy(kernel_hbm, kernel, k_sem)
    weights.start()

    def send(src, dst, send_sem, recv_sem, target):
        copy = pltpu.make_async_remote_copy(
            src_ref=src, dst_ref=dst, send_sem=send_sem, recv_sem=recv_sem,
            device_id=target, device_id_type=MESH,
        )
        copy.start()
        return copy

    def total(*terms):
        result = terms[0].astype(F32)
        for term in terms[1:]:
            result += term.astype(F32)
        return result

    lines[:, 120:128, :] = jnp.zeros((4, 8, 128), F32)
    col = lax.broadcasted_iota(jnp.int32, (cols, C), 0)

    def put(f, r, plain):
        wide = plain.astype(F32)
        wins[0, f, r] = jnp.where(col == cols - 1, 0.0, pltpu.roll(wide, cols - 1, 0)).astype(BF16)
        wins[1, f, r] = wide.astype(BF16)
        wins[2, f, r] = jnp.where(col == 0, 0.0, pltpu.roll(wide, 1, 0)).astype(BF16)

    def own_row(index, carry):
        f, r = lax.div(index, rows), lax.rem(index, rows)
        put(f, r + 1, cot[f, r])
        return carry

    lax.fori_loop(0, frames * rows, own_row, 0)

    def norm():
        wide = video[...].reshape(pixels, C).astype(F32)
        inverse = lax.rsqrt(jnp.mean(wide * wide, axis=-1, keepdims=True) + 1e-6)
        normed = wide * inverse * gain[...]
        return wide, inverse, normed, 1.0 / (1.0 + jnp.exp(-normed))

    _, _, normed, gate = norm()
    hid_t[...] = (normed * gate).astype(BF16).astype(F32).T.astype(BF16)

    pl.semaphore_wait(barrier, len(peers))
    for r in (NEAR, 16 - NEAR):
        pl.semaphore_signal(
            far_sem, inc=1, device_id=device(y, turn(z, r, 16), x, core), device_id_type=MESH
        )
    halo = [
        (cot.at[0:2], ext.at[4:6, 1:3], (prev_t, s)),
        (cot.at[0:2, rows - 1], ext.at[4:6, 0], (prev_t, down)),
        (cot.at[0:2, 0], ext.at[4:6, 3], (prev_t, up)),
        (cot.at[:, rows - 1], ext.at[0:4, 0], (t, down)),
        (cot.at[:, 0], ext.at[0:4, 3], (t, up)),
    ]
    halo = [send(a, b, h_send.at[i], h_recv.at[i], d) for i, (a, b, d) in enumerate(halo)]

    def window(tap):
        a, b, d = tap // 9, tap // 3 % 3, tap % 3
        block = wins[d, 2 - a : 2 - a + frames, 2 - b : 2 - b + rows]
        return block.reshape(pixels, C)

    def kernel_term(tap):
        term = jnp.dot(hid_t[...], window(tap), preferred_element_type=F32)
        klow[tap * C : (tap + 1) * C, :] = term[:, :128]
        khigh[tap * C : (tap + 1) * C, 0:64] = term[:, 128:]

    def hidden_term(tap, first=False):
        term = lax.dot_general(
            window(tap), kernel[tap], (((1,), (1,)), ((), ())), preferred_element_type=F32
        )
        if first:
            acc[...] = term
        else:
            acc[...] += term

    local_taps = (21, 22, 23)
    for tap in local_taps:
        kernel_term(tap)
    for copy in halo:
        copy.wait_recv()

    def far_row(index, carry):
        f, r = lax.div(index, 2), lax.rem(index, 2) * 3
        gone = ((r == 0) & (s == 0)) | ((r == 3) & (s == n_s - 1)) | ((f >= 4) & (t == n_t - 1))
        put(f, r, jnp.where(gone, 0.0, ext[f, r].astype(F32)))
        return carry

    def late_row(index, carry):
        f, r = lax.div(index, 2) + 4, lax.rem(index, 2) + 1
        put(f, r, jnp.where(t == n_t - 1, 0.0, ext[f, r].astype(F32)))
        return carry

    lax.fori_loop(0, 12, far_row, 0)
    lax.fori_loop(0, 4, late_row, 0)

    def pack(quarter):
        for where in range(16):
            row = (quarter * 16 + where) * 81
            buf = lines.at[where % 4]
            even, odd = pl.ds(row, 41, stride=2), pl.ds(row + 1, 40, stride=2)
            even_high = khigh[even, :]
            turned = pltpu.roll(klow[odd, :], 64, 1)
            left = lax.broadcasted_iota(jnp.int32, (40, 128), 1) < 64
            buf[pl.ds(0, 41, stride=3), :] = klow[even, :]
            buf[pl.ds(1, 40, stride=3), :] = jnp.where(left, even_high[:40], turned)
            buf[pl.ds(2, 40, stride=3), :] = jnp.where(left, turned, pltpu.roll(khigh[odd, :], 64, 1))
            buf[121:122, :] = jnp.where(left[:1], even_high[40:41], 0.0)
            lane = lax.broadcasted_iota(jnp.int32, (16, 128), 1)
            for m in range(8):
                start, skip = 15 * m + 24 * m // 128, 24 * m % 128
                tile = buf[start : start + 16, :]
                if skip:
                    tile = jnp.where(
                        lane < 128 - skip,
                        pltpu.roll(tile, 128 - skip, 1),
                        pltpu.roll(buf[start + 1 : start + 17, :], 128 - skip, 1),
                    )
                packed[m % 2, m // 2, quarter, where] = tile.astype(BF16)

    order = (1, 3, 2)
    other = 1 - core
    partner = device(y, z, x, other)
    pair_copies, x_copies, y_copies = {}, {}, {}

    def pair_stage(quarter):
        pair_copies[quarter].wait_recv()
        for r in order:
            xt = turn(x, r, 4)
            i = quarter * 3 + r - 1
            sx[r - 1, quarter] = total(packed[core, xt, quarter, 0:XZ], rc[quarter, xt, 0:XZ]).astype(BF16)
            x_copies[r, quarter] = send(
                sx.at[r - 1, quarter], rx.at[r - 1, quarter], x_send.at[i], x_recv.at[i], device(y, z, xt, core)
            )

    done = 0
    for quarter in range(4):
        until = (7, 14, 21, 27)[quarter]
        for tap in range(done, until):
            if tap not in local_taps:
                kernel_term(tap)
        done = until
        pack(quarter)
        pair_copies[quarter] = send(
            packed.at[other, :, quarter], rc.at[quarter], c_send.at[quarter], c_recv.at[quarter], partner
        )
        if quarter:
            pair_stage(quarter - 1)
    weights.wait()
    early = 4
    for tap in range(early):
        hidden_term(tap, tap == 0)
    pair_stage(3)
    for r in order:
        yt = turn(y, r, 4)
        sy[r - 1] = total(packed[core, :, yt, XZ:16], rc[yt, :, XZ:16]).astype(BF16)
        y_copies[r] = send(
            sy.at[r - 1], ry.at[r - 1], y_send.at[r - 1], y_recv.at[r - 1], device(turn(y, r, 4), z, x, core)
        )
    for tap in range(early, TAPS):
        hidden_term(tap)
    wide, inverse, normed, gate = norm()
    ngrad = acc[...] * gate * (1.0 + normed * (1.0 - gate))
    gain_sum = jnp.sum(ngrad * wide * inverse, axis=0, keepdims=True)
    g1[0:1, :] = gain_sum[:, :128]
    g1[1:2, :] = jnp.concatenate([gain_sum[:, 128:], jnp.zeros((1, 64), F32)], axis=1)
    gain_copies = [
        send(g1, q1.at[r - 1], q1_send.at[r - 1], q1_recv.at[r - 1], mate(r)) for r in range(1, 8)
    ]
    scaled = ngrad * gain[...]
    mean = jnp.mean(scaled * wide, axis=-1, keepdims=True)
    result = inverse * scaled - wide * (inverse * inverse * inverse) * mean
    vgrad[...] = result.astype(BF16).reshape(video.shape)

    for copy in x_copies.values():
        copy.wait_recv()
    for copy in y_copies.values():
        copy.wait_recv()

    def part_x(yt):
        return total(packed[core, x, yt, 0:XZ], rc[yt, x, 0:XZ], rx[0, yt], rx[1, yt], rx[2, yt])

    def part_y(xt):
        return total(packed[core, xt, y, XZ:16], rc[y, xt, XZ:16], ry[0, xt], ry[1, xt], ry[2, xt])

    second = {}
    for r in order:
        xt, yt = turn(x, r, 4), turn(y, r, 4)
        sy2[r - 1] = part_x(yt).astype(BF16)
        second[r, 0] = send(
            sy2.at[r - 1], ry2.at[r - 1], b_send.at[r - 1], b_recv.at[r - 1], device(yt, z, x, core)
        )
        sx2[r - 1] = part_y(xt).astype(BF16)
        second[r, 1] = send(
            sx2.at[r - 1], rx2.at[r - 1], b_send.at[r + 2], b_recv.at[r + 2], device(y, z, xt, core)
        )
    for copy in gain_copies:
        copy.wait_recv()
    g2[...] = total(g1[...], *(q1[r] for r in range(7)))
    gain_second = [
        send(g2, q2.at[r - 1], q2_send.at[r - 1], q2_recv.at[r - 1], device(turn(y, r, 4), z, x, core))
        for r in range(1, 4)
    ]
    own_x, own_y = part_x(y), part_y(x)
    for copy in second.values():
        copy.wait_recv()
    s3[0:XZ] = total(own_x, ry2[0], ry2[1], ry2[2]).astype(BF16)
    s3[XZ:16] = total(own_y, rx2[0], rx2[1], rx2[2]).astype(BF16)
    pl.semaphore_wait(far_sem, 2)
    third, gain_third = [], []
    hops = (8, 7, 9, 6, 10, 5, 11, 4, 12, 3, 13, 2, 14, 1, 15)
    for r in hops:
        zt = turn(z, r, 16)
        third.append(
            send(s3.at[zt], r3.at[r - 1], z_send.at[r - 1], z_recv.at[r - 1], device(y, zt, x, core))
        )
    for copy in gain_second:
        copy.wait_recv()
    g3[...] = total(g2[...], *(q2[r] for r in range(3)))
    for r in hops:
        gain_third.append(
            send(g3, q3.at[r - 1], q3_send.at[r - 1], q3_recv.at[r - 1], device(y, turn(z, r, 16), x, core))
        )
    for copy in third:
        copy.wait_recv()
    final = total(s3[z], *(r3[r] for r in range(15))) * (1.0 / 512)
    out[...] = final
    for copy in gain_third:
        copy.wait_recv()
    gain_out[...] = total(g3[...], *(q3[r] for r in range(15))) * (1.0 / 512)
    for group in (
        halo, pair_copies.values(), x_copies.values(), y_copies.values(), gain_copies,
        second.values(), gain_second, third, gain_third,
    ):
        for copy in group:
            copy.wait_send()


def fused(video, gain, kernel, cot):
    frames, rows, cols, _ = video.shape
    pixels = frames * rows * cols
    vmem = pl.BlockSpec(memory_space=pltpu.VMEM)

    def tiles(*shape):
        return pltpu.VMEM(shape + (16, 128), BF16)

    def line(*shape):
        return pltpu.VMEM(shape + (2, 128), F32)

    def dma(count):
        return [pltpu.SemaphoreType.DMA((count,))] * 2

    return pl.pallas_call(
        fused_kernel,
        out_shape=(
            jax.ShapeDtypeStruct(video.shape, BF16),
            jax.ShapeDtypeStruct((16, 128), F32),
            jax.ShapeDtypeStruct((2, 128), F32),
        ),
        in_specs=[vmem, vmem, pl.BlockSpec(memory_space=pl.ANY), vmem],
        out_specs=(vmem, vmem, vmem),
        scratch_shapes=[
            pltpu.VMEM((TAPS, C, C), BF16),
            pltpu.VMEM((frames + 2, rows + 2, cols, C), BF16),
            pltpu.VMEM((3, frames + 2, rows + 2, cols, C), BF16),
            pltpu.VMEM((C, pixels), BF16),
            pltpu.VMEM((TAPS * C, 128), F32),
            pltpu.VMEM((TAPS * C, 128), F32),
            pltpu.VMEM((4, 128, 128), F32),
            pltpu.VMEM((pixels, C), F32),
            tiles(2, 4, 4, 16),
            tiles(4, 4, 16),
            tiles(3, 4, XZ), tiles(3, 4, XZ), tiles(3, 4, 16 - XZ), tiles(3, 4, 16 - XZ),
            tiles(3, 16 - XZ), tiles(3, 16 - XZ), tiles(3, XZ), tiles(3, XZ),
            tiles(16), tiles(15),
            line(), line(7), line(), line(3), line(), line(15),
            pltpu.SemaphoreType.DMA, pltpu.SemaphoreType.REGULAR,
            *dma(5), *dma(4), *dma(12), *dma(3), *dma(6), *dma(15),
            *dma(7), *dma(3), *dma(15),
        ],
        compiler_params=pltpu.CompilerParams(
            collective_id=0, has_side_effects=True, vmem_limit_bytes=32 << 20
        ),
        name="fused_backward",
    )(video, gain.reshape(1, C), kernel.reshape(TAPS, C, C), cot)


def finish_kernel(vgrad, tile, gain_rows, vgrad_out, share, gain_out):
    vgrad_out[...] = vgrad[...]
    gain_out[0:128] = gain_rows[0]
    gain_out[128:C] = gain_rows[1, : C - 128]
    for a in range(15):
        share[128 * a : 128 * a + 128] = tile[a]
    share[1920:1944] = tile[15, :24]


def finish(vgrad, tile, gain_rows):
    vmem = pl.BlockSpec(memory_space=pltpu.VMEM)
    return pl.pallas_call(
        finish_kernel,
        out_shape=(
            jax.ShapeDtypeStruct(vgrad.shape, BF16),
            jax.ShapeDtypeStruct((1944,), F32),
            jax.ShapeDtypeStruct((C,), F32),
        ),
        in_specs=[vmem] * 3,
        out_specs=(vmem,) * 3,
        compiler_params=pltpu.CompilerParams(vmem_limit_bytes=8 << 20),
        name="finish",
    )(vgrad, tile, gain_rows)


def on_device(video, gain, kernel, cotangent):
    return finish(*fused(video, gain, kernel, cotangent))


def solution(mesh):
    in_specs = (P("tm", "space", None, None), P(), P(), P("tm", "space", None, None))
    out_specs = (P("tm", "space", None, None), P(("tm", "space")), P())
    return jax.shard_map(
        on_device, mesh=mesh, in_specs=in_specs, out_specs=out_specs, check_vma=False
    )
```

```python
import jax
import jax.numpy as jnp
from jax import lax
from jax.experimental import pallas as pl
from jax.experimental.pallas import tpu as pltpu
from jax.sharding import PartitionSpec as P

F32 = jnp.float32
BF16 = jnp.bfloat16
C = 192
TAPS = 27
MESH = pl.DeviceIdType.MESH
XZ = 10
NEAR = 4


def fused_kernel(
    video_hbm, gain_hbm, kernel_hbm, cot_hbm, vgrad, out, gain_out,
    video, gain, cot, kernel, ext, wins, hid_t, klow, khigh, lines, acc, packed,
    rc, sx, rx, sy, ry, sx2, rx2, sy2, ry2, s3, r3, g1, q1, g2, q2, g3, q3,
    v_sem, n_sem, o_sem, k_sem, far_sem, h_send, h_recv, c_send, c_recv, x_send, x_recv, y_send, y_recv,
    b_send, b_recv, z_send, z_recv,
    q1_send, q1_recv, q2_send, q2_recv, q3_send, q3_recv,
):
    frames, rows, cols, _ = video.shape
    pixels = frames * rows * cols
    t, s = lax.axis_index("tm"), lax.axis_index("space")
    n_t, n_s = lax.axis_size("tm"), lax.axis_size("space")
    y, z, x = lax.div(t, 32), lax.rem(lax.div(t, 2), 16), lax.rem(t, 2) * 2 + lax.div(s, 2)
    core = lax.rem(s, 2)
    member = x * 2 + core

    def device(y, z, x, core):
        return ((y * 16 + z) * 2 + lax.div(x, 2), lax.rem(x, 2) * 2 + core)

    def turn(index, r, n):
        return lax.rem(index + r, n)

    def mate(r):
        m = turn(member, r, 8)
        return device(y, z, lax.div(m, 2), lax.rem(m, 2))

    next_t, prev_t = turn(t, 1, n_t), turn(t, n_t - 1, n_t)
    up, down = turn(s, n_s - 1, n_s), turn(s, 1, n_s)
    peers = [mate(r) for r in range(1, 8)]
    peers += [device(turn(y, r, 4), z, x, core) for r in range(1, 4)]
    peers += [device(y, turn(z, r, 16), x, core) for r in range(1, 16) if min(r, 16 - r) <= NEAR]
    peers += [(next_t, s), (next_t, up), (next_t, down), (t, up), (t, down)]
    barrier = pltpu.get_barrier_semaphore()
    for peer in peers:
        pl.semaphore_signal(barrier, inc=1, device_id=peer, device_id_type=MESH)
    cot_in = pltpu.make_async_copy(cot_hbm, cot, o_sem)
    video_in = pltpu.make_async_copy(video_hbm, video, v_sem)
    gain_in = pltpu.make_async_copy(gain_hbm, gain, n_sem)
    weights = pltpu.make_async_copy(kernel_hbm, kernel, k_sem)
    for copy in (cot_in, video_in, gain_in, weights):
        copy.start()

    def send(src, dst, send_sem, recv_sem, target):
        copy = pltpu.make_async_remote_copy(
            src_ref=src, dst_ref=dst, send_sem=send_sem, recv_sem=recv_sem,
            device_id=target, device_id_type=MESH,
        )
        copy.start()
        return copy

    def total(*terms):
        result = terms[0].astype(F32)
        for term in terms[1:]:
            result += term.astype(F32)
        return result

    lines[:, 120:128, :] = jnp.zeros((4, 8, 128), F32)
    col = lax.broadcasted_iota(jnp.int32, (cols, C), 0)

    def put(f, r, plain):
        wide = plain.astype(F32)
        wins[0, f, r] = jnp.where(col == cols - 1, 0.0, pltpu.roll(wide, cols - 1, 0)).astype(BF16)
        wins[1, f, r] = wide.astype(BF16)
        wins[2, f, r] = jnp.where(col == 0, 0.0, pltpu.roll(wide, 1, 0)).astype(BF16)

    def own_row(index, carry):
        f, r = lax.div(index, rows), lax.rem(index, rows)
        put(f, r + 1, cot[f, r])
        return carry

    cot_in.wait()
    lax.fori_loop(0, frames * rows, own_row, 0)
    video_in.wait()
    gain_in.wait()

    def norm():
        wide = video[...].reshape(pixels, C).astype(F32)
        inverse = lax.rsqrt(jnp.mean(wide * wide, axis=-1, keepdims=True) + 1e-6)
        normed = wide * inverse * gain[...]
        return wide, inverse, normed, 1.0 / (1.0 + jnp.exp(-normed))

    _, _, normed, gate = norm()
    hid_t[...] = (normed * gate).astype(BF16).astype(F32).T.astype(BF16)

    pl.semaphore_wait(barrier, len(peers))
    for r in (NEAR, 16 - NEAR):
        pl.semaphore_signal(
            far_sem, inc=1, device_id=device(y, turn(z, r, 16), x, core), device_id_type=MESH
        )
    halo = [
        (cot.at[0:2], ext.at[4:6, 1:3], (prev_t, s)),
        (cot.at[0:2, rows - 1], ext.at[4:6, 0], (prev_t, down)),
        (cot.at[0:2, 0], ext.at[4:6, 3], (prev_t, up)),
        (cot.at[:, rows - 1], ext.at[0:4, 0], (t, down)),
        (cot.at[:, 0], ext.at[0:4, 3], (t, up)),
    ]
    halo = [send(a, b, h_send.at[i], h_recv.at[i], d) for i, (a, b, d) in enumerate(halo)]

    def window(tap):
        a, b, d = tap // 9, tap // 3 % 3, tap % 3
        block = wins[d, 2 - a : 2 - a + frames, 2 - b : 2 - b + rows]
        return block.reshape(pixels, C)

    def kernel_term(tap):
        term = jnp.dot(hid_t[...], window(tap), preferred_element_type=F32)
        klow[tap * C : (tap + 1) * C, :] = term[:, :128]
        khigh[tap * C : (tap + 1) * C, 0:64] = term[:, 128:]

    def hidden_term(tap, first=False):
        term = lax.dot_general(
            window(tap), kernel[tap], (((1,), (1,)), ((), ())), preferred_element_type=F32
        )
        if first:
            acc[...] = term
        else:
            acc[...] += term

    local_taps = (21, 22, 23)
    for tap in local_taps:
        kernel_term(tap)
    for copy in halo:
        copy.wait_recv()

    def far_row(index, carry):
        f, r = lax.div(index, 2), lax.rem(index, 2) * 3
        gone = ((r == 0) & (s == 0)) | ((r == 3) & (s == n_s - 1)) | ((f >= 4) & (t == n_t - 1))
        put(f, r, jnp.where(gone, 0.0, ext[f, r].astype(F32)))
        return carry

    def late_row(index, carry):
        f, r = lax.div(index, 2) + 4, lax.rem(index, 2) + 1
        put(f, r, jnp.where(t == n_t - 1, 0.0, ext[f, r].astype(F32)))
        return carry

    lax.fori_loop(0, 12, far_row, 0)
    lax.fori_loop(0, 4, late_row, 0)

    def pack(quarter):
        for where in range(16):
            row = (quarter * 16 + where) * 81
            buf = lines.at[where % 4]
            even, odd = pl.ds(row, 41, stride=2), pl.ds(row + 1, 40, stride=2)
            even_high = khigh[even, :]
            turned = pltpu.roll(klow[odd, :], 64, 1)
            left = lax.broadcasted_iota(jnp.int32, (40, 128), 1) < 64
            buf[pl.ds(0, 41, stride=3), :] = klow[even, :]
            buf[pl.ds(1, 40, stride=3), :] = jnp.where(left, even_high[:40], turned)
            buf[pl.ds(2, 40, stride=3), :] = jnp.where(left, turned, pltpu.roll(khigh[odd, :], 64, 1))
            buf[121:122, :] = jnp.where(left[:1], even_high[40:41], 0.0)
            lane = lax.broadcasted_iota(jnp.int32, (16, 128), 1)
            for m in range(8):
                start, skip = 15 * m + 24 * m // 128, 24 * m % 128
                tile = buf[start : start + 16, :]
                if skip:
                    tile = jnp.where(
                        lane < 128 - skip,
                        pltpu.roll(tile, 128 - skip, 1),
                        pltpu.roll(buf[start + 1 : start + 17, :], 128 - skip, 1),
                    )
                packed[m % 2, m // 2, quarter, where] = tile.astype(BF16)

    order = (1, 3, 2)
    other = 1 - core
    partner = device(y, z, x, other)
    pair_copies, x_copies, y_copies = {}, {}, {}

    def pair_stage(quarter):
        pair_copies[quarter].wait_recv()
        for r in order:
            xt = turn(x, r, 4)
            i = quarter * 3 + r - 1
            sx[r - 1, quarter] = total(packed[core, xt, quarter, 0:XZ], rc[quarter, xt, 0:XZ]).astype(BF16)
            x_copies[r, quarter] = send(
                sx.at[r - 1, quarter], rx.at[r - 1, quarter], x_send.at[i], x_recv.at[i], device(y, z, xt, core)
            )

    done = 0
    for quarter in range(4):
        until = (7, 14, 21, 27)[quarter]
        for tap in range(done, until):
            if tap not in local_taps:
                kernel_term(tap)
        done = until
        pack(quarter)
        pair_copies[quarter] = send(
            packed.at[other, :, quarter], rc.at[quarter], c_send.at[quarter], c_recv.at[quarter], partner
        )
        if quarter:
            pair_stage(quarter - 1)
    weights.wait()
    early = 4
    for tap in range(early):
        hidden_term(tap, tap == 0)
    pair_stage(3)
    for r in order:
        yt = turn(y, r, 4)
        sy[r - 1] = total(packed[core, :, yt, XZ:16], rc[yt, :, XZ:16]).astype(BF16)
        y_copies[r] = send(
            sy.at[r - 1], ry.at[r - 1], y_send.at[r - 1], y_recv.at[r - 1], device(turn(y, r, 4), z, x, core)
        )
    for tap in range(early, TAPS):
        hidden_term(tap)
    wide, inverse, normed, gate = norm()
    ngrad = acc[...] * gate * (1.0 + normed * (1.0 - gate))
    gain_sum = jnp.sum(ngrad * wide * inverse, axis=0, keepdims=True)
    g1[0:1, :] = gain_sum[:, :128]
    g1[1:2, :] = jnp.concatenate([gain_sum[:, 128:], jnp.zeros((1, 64), F32)], axis=1)
    gain_copies = [
        send(g1, q1.at[r - 1], q1_send.at[r - 1], q1_recv.at[r - 1], mate(r)) for r in range(1, 8)
    ]
    scaled = ngrad * gain[...]
    mean = jnp.mean(scaled * wide, axis=-1, keepdims=True)
    result = inverse * scaled - wide * (inverse * inverse * inverse) * mean
    vgrad[...] = result.astype(BF16).reshape(video.shape)

    for copy in x_copies.values():
        copy.wait_recv()
    for copy in y_copies.values():
        copy.wait_recv()

    def part_x(yt):
        return total(packed[core, x, yt, 0:XZ], rc[yt, x, 0:XZ], rx[0, yt], rx[1, yt], rx[2, yt])

    def part_y(xt):
        return total(packed[core, xt, y, XZ:16], rc[y, xt, XZ:16], ry[0, xt], ry[1, xt], ry[2, xt])

    second = {}
    for r in order:
        xt, yt = turn(x, r, 4), turn(y, r, 4)
        sy2[r - 1] = part_x(yt).astype(BF16)
        second[r, 0] = send(
            sy2.at[r - 1], ry2.at[r - 1], b_send.at[r - 1], b_recv.at[r - 1], device(yt, z, x, core)
        )
        sx2[r - 1] = part_y(xt).astype(BF16)
        second[r, 1] = send(
            sx2.at[r - 1], rx2.at[r - 1], b_send.at[r + 2], b_recv.at[r + 2], device(y, z, xt, core)
        )
    for copy in gain_copies:
        copy.wait_recv()
    g2[...] = total(g1[...], *(q1[r] for r in range(7)))
    gain_second = [
        send(g2, q2.at[r - 1], q2_send.at[r - 1], q2_recv.at[r - 1], device(turn(y, r, 4), z, x, core))
        for r in range(1, 4)
    ]
    own_x, own_y = part_x(y), part_y(x)
    for copy in second.values():
        copy.wait_recv()
    s3[0:XZ] = total(own_x, ry2[0], ry2[1], ry2[2]).astype(BF16)
    s3[XZ:16] = total(own_y, rx2[0], rx2[1], rx2[2]).astype(BF16)
    pl.semaphore_wait(far_sem, 2)
    third, gain_third = [], []
    hops = (8, 7, 9, 6, 10, 5, 11, 4, 12, 3, 13, 2, 14, 1, 15)
    for r in hops:
        zt = turn(z, r, 16)
        third.append(
            send(s3.at[zt], r3.at[r - 1], z_send.at[r - 1], z_recv.at[r - 1], device(y, zt, x, core))
        )
    for copy in gain_second:
        copy.wait_recv()
    g3[...] = total(g2[...], *(q2[r] for r in range(3)))
    for r in hops:
        gain_third.append(
            send(g3, q3.at[r - 1], q3_send.at[r - 1], q3_recv.at[r - 1], device(y, turn(z, r, 16), x, core))
        )
    for copy in third:
        copy.wait_recv()
    final = total(s3[z], *(r3[r] for r in range(15))) * (1.0 / 512)
    out[...] = final
    for copy in gain_third:
        copy.wait_recv()
    gain_out[...] = total(g3[...], *(q3[r] for r in range(15))) * (1.0 / 512)
    for group in (
        halo, pair_copies.values(), x_copies.values(), y_copies.values(), gain_copies,
        second.values(), gain_second, third, gain_third,
    ):
        for copy in group:
            copy.wait_send()


def fused(video, gain, kernel, cot):
    frames, rows, cols, _ = video.shape
    pixels = frames * rows * cols
    vmem = pl.BlockSpec(memory_space=pltpu.VMEM)

    def tiles(*shape):
        return pltpu.VMEM(shape + (16, 128), BF16)

    def line(*shape):
        return pltpu.VMEM(shape + (2, 128), F32)

    def dma(count):
        return [pltpu.SemaphoreType.DMA((count,))] * 2

    return pl.pallas_call(
        fused_kernel,
        out_shape=(
            pltpu.VMEM(video.shape, BF16),
            pltpu.VMEM((16, 128), F32),
            pltpu.VMEM((2, 128), F32),
        ),
        in_specs=[pl.BlockSpec(memory_space=pl.ANY)] * 4,
        out_specs=(vmem, vmem, vmem),
        scratch_shapes=[
            pltpu.VMEM(video.shape, BF16),
            pltpu.VMEM((1, C), F32),
            pltpu.VMEM(cot.shape, BF16),
            pltpu.VMEM((TAPS, C, C), BF16),
            pltpu.VMEM((frames + 2, rows + 2, cols, C), BF16),
            pltpu.VMEM((3, frames + 2, rows + 2, cols, C), BF16),
            pltpu.VMEM((C, pixels), BF16),
            pltpu.VMEM((TAPS * C, 128), F32),
            pltpu.VMEM((TAPS * C, 128), F32),
            pltpu.VMEM((4, 128, 128), F32),
            pltpu.VMEM((pixels, C), F32),
            tiles(2, 4, 4, 16),
            tiles(4, 4, 16),
            tiles(3, 4, XZ), tiles(3, 4, XZ), tiles(3, 4, 16 - XZ), tiles(3, 4, 16 - XZ),
            tiles(3, 16 - XZ), tiles(3, 16 - XZ), tiles(3, XZ), tiles(3, XZ),
            tiles(16), tiles(15),
            line(), line(7), line(), line(3), line(), line(15),
            *[pltpu.SemaphoreType.DMA] * 4, pltpu.SemaphoreType.REGULAR,
            *dma(5), *dma(4), *dma(12), *dma(3), *dma(6), *dma(15),
            *dma(7), *dma(3), *dma(15),
        ],
        compiler_params=pltpu.CompilerParams(
            collective_id=0, has_side_effects=True, vmem_limit_bytes=59 << 20
        ),
        name="fused_backward",
    )(video, gain.reshape(1, C), kernel.reshape(TAPS, C, C), cot)


def finish_kernel(vgrad, tile, gain_rows, vgrad_out, share, gain_out):
    vgrad_out[...] = vgrad[...]
    gain_out[0:128] = gain_rows[0]
    gain_out[128:C] = gain_rows[1, : C - 128]
    for a in range(15):
        share[128 * a : 128 * a + 128] = tile[a]
    share[1920:1944] = tile[15, :24]


def finish(vgrad, tile, gain_rows):
    vmem = pl.BlockSpec(memory_space=pltpu.VMEM)
    return pl.pallas_call(
        finish_kernel,
        out_shape=(
            jax.ShapeDtypeStruct(vgrad.shape, BF16),
            jax.ShapeDtypeStruct((1944,), F32),
            jax.ShapeDtypeStruct((C,), F32),
        ),
        in_specs=[vmem] * 3,
        out_specs=(vmem,) * 3,
        compiler_params=pltpu.CompilerParams(vmem_limit_bytes=8 << 20),
        name="finish",
    )(vgrad, tile, gain_rows)


def on_device(video, gain, kernel, cotangent):
    return finish(*fused(video, gain, kernel, cotangent))


def solution(mesh):
    in_specs = (P("tm", "space", None, None), P(), P(), P("tm", "space", None, None))
    out_specs = (P("tm", "space", None, None), P(("tm", "space")), P())
    return jax.shard_map(
        on_device, mesh=mesh, in_specs=in_specs, out_specs=out_specs, check_vma=False
    )
```

```python
import jax
import jax.numpy as jnp
from jax import lax
from jax.experimental import pallas as pl
from jax.experimental.pallas import tpu as pltpu
from jax.sharding import PartitionSpec as P

F32 = jnp.float32
BF16 = jnp.bfloat16
C = 192
TAPS = 27
MESH = pl.DeviceIdType.MESH
XZ = 10
NEAR = 4


def fused_kernel(
    video_hbm, gain_hbm, kernel_hbm, cot_hbm, vgrad, out, gain_out,
    video, gain, cot, kernel, ext, wins, hid_t, klow, khigh, lines, acc, packed,
    rc, sx, rx, sy, ry, sx2, rx2, sy2, ry2, s3, r3, g1, q1, g2, q2, g3, q3,
    v_sem, n_sem, o_sem, k_sem, far_sem, h_send, h_recv, c_send, c_recv, x_send, x_recv, y_send, y_recv,
    b_send, b_recv, z_send, z_recv,
    q1_send, q1_recv, q2_send, q2_recv, q3_send, q3_recv,
):
    frames, rows, cols, _ = video.shape
    pixels = frames * rows * cols
    t, s = lax.axis_index("tm"), lax.axis_index("space")
    n_t, n_s = lax.axis_size("tm"), lax.axis_size("space")
    y, z, x = lax.div(t, 32), lax.rem(lax.div(t, 2), 16), lax.rem(t, 2) * 2 + lax.div(s, 2)
    core = lax.rem(s, 2)
    member = x * 2 + core

    def device(y, z, x, core):
        return ((y * 16 + z) * 2 + lax.div(x, 2), lax.rem(x, 2) * 2 + core)

    def turn(index, r, n):
        return lax.rem(index + r, n)

    def mate(r):
        m = turn(member, r, 8)
        return device(y, z, lax.div(m, 2), lax.rem(m, 2))

    next_t, prev_t = turn(t, 1, n_t), turn(t, n_t - 1, n_t)
    up, down = turn(s, n_s - 1, n_s), turn(s, 1, n_s)
    peers = [mate(r) for r in range(1, 8)]
    peers += [device(turn(y, r, 4), z, x, core) for r in range(1, 4)]
    peers += [device(y, turn(z, r, 16), x, core) for r in range(1, 16) if min(r, 16 - r) <= NEAR]
    peers += [(next_t, s), (next_t, up), (next_t, down), (t, up), (t, down)]
    barrier = pltpu.get_barrier_semaphore()
    for peer in peers:
        pl.semaphore_signal(barrier, inc=1, device_id=peer, device_id_type=MESH)
    cot_in = pltpu.make_async_copy(cot_hbm, cot, o_sem)
    video_in = pltpu.make_async_copy(video_hbm, video, v_sem)
    gain_in = pltpu.make_async_copy(gain_hbm, gain, n_sem)
    weights = pltpu.make_async_copy(kernel_hbm, kernel, k_sem)
    for copy in (cot_in, video_in, gain_in, weights):
        copy.start()

    def send(src, dst, send_sem, recv_sem, target):
        copy = pltpu.make_async_remote_copy(
            src_ref=src, dst_ref=dst, send_sem=send_sem, recv_sem=recv_sem,
            device_id=target, device_id_type=MESH,
        )
        copy.start()
        return copy

    def total(*terms):
        result = terms[0].astype(F32)
        for term in terms[1:]:
            result += term.astype(F32)
        return result

    lines[:, 120:128, :] = jnp.zeros((4, 8, 128), F32)
    col = lax.broadcasted_iota(jnp.int32, (cols, C), 0)

    def put(f, r, plain):
        wide = plain.astype(F32)
        wins[0, f, r] = jnp.where(col == cols - 1, 0.0, pltpu.roll(wide, cols - 1, 0)).astype(BF16)
        wins[1, f, r] = wide.astype(BF16)
        wins[2, f, r] = jnp.where(col == 0, 0.0, pltpu.roll(wide, 1, 0)).astype(BF16)

    def own_row(index, carry):
        f, r = lax.div(index, rows), lax.rem(index, rows)
        put(f, r + 1, cot[f, r])
        return carry

    cot_in.wait()
    lax.fori_loop(0, frames * rows, own_row, 0)
    video_in.wait()
    gain_in.wait()

    def norm():
        wide = video[...].reshape(pixels, C).astype(F32)
        inverse = lax.rsqrt(jnp.mean(wide * wide, axis=-1, keepdims=True) + 1e-6)
        normed = wide * inverse * gain[...]
        return wide, inverse, normed, 1.0 / (1.0 + jnp.exp(-normed))

    _, _, normed, gate = norm()
    hid_t[...] = (normed * gate).astype(BF16).astype(F32).T.astype(BF16)

    pl.semaphore_wait(barrier, len(peers))
    for r in (NEAR, 16 - NEAR):
        pl.semaphore_signal(
            far_sem, inc=1, device_id=device(y, turn(z, r, 16), x, core), device_id_type=MESH
        )
    halo = [
        (cot.at[0:2], ext.at[4:6, 1:3], (prev_t, s)),
        (cot.at[0:2, rows - 1], ext.at[4:6, 0], (prev_t, down)),
        (cot.at[0:2, 0], ext.at[4:6, 3], (prev_t, up)),
        (cot.at[:, rows - 1], ext.at[0:4, 0], (t, down)),
        (cot.at[:, 0], ext.at[0:4, 3], (t, up)),
    ]
    halo = [send(a, b, h_send.at[i], h_recv.at[i], d) for i, (a, b, d) in enumerate(halo)]

    def window(tap):
        a, b, d = tap // 9, tap // 3 % 3, tap % 3
        block = wins[d, 2 - a : 2 - a + frames, 2 - b : 2 - b + rows]
        return block.reshape(pixels, C)

    def kernel_term(tap):
        term = jnp.dot(hid_t[...], window(tap), preferred_element_type=F32)
        klow[tap * C : (tap + 1) * C, :] = term[:, :128]
        khigh[tap * C : (tap + 1) * C, 0:64] = term[:, 128:]

    def hidden_term(tap, first=False):
        term = lax.dot_general(
            window(tap), kernel[tap], (((1,), (1,)), ((), ())), preferred_element_type=F32
        )
        if first:
            acc[...] = term
        else:
            acc[...] += term

    local_taps = (21, 22, 23)
    for tap in local_taps:
        kernel_term(tap)
    for copy in halo:
        copy.wait_recv()

    def far_row(index, carry):
        f, r = lax.div(index, 2), lax.rem(index, 2) * 3
        gone = ((r == 0) & (s == 0)) | ((r == 3) & (s == n_s - 1)) | ((f >= 4) & (t == n_t - 1))
        put(f, r, jnp.where(gone, 0.0, ext[f, r].astype(F32)))
        return carry

    def late_row(index, carry):
        f, r = lax.div(index, 2) + 4, lax.rem(index, 2) + 1
        put(f, r, jnp.where(t == n_t - 1, 0.0, ext[f, r].astype(F32)))
        return carry

    lax.fori_loop(0, 12, far_row, 0)
    lax.fori_loop(0, 4, late_row, 0)

    def pack(quarter):
        for where in range(16):
            row = (quarter * 16 + where) * 81
            buf = lines.at[where % 4]
            even, odd = pl.ds(row, 41, stride=2), pl.ds(row + 1, 40, stride=2)
            even_high = khigh[even, :]
            turned = pltpu.roll(klow[odd, :], 64, 1)
            left = lax.broadcasted_iota(jnp.int32, (40, 128), 1) < 64
            buf[pl.ds(0, 41, stride=3), :] = klow[even, :]
            buf[pl.ds(1, 40, stride=3), :] = jnp.where(left, even_high[:40], turned)
            buf[pl.ds(2, 40, stride=3), :] = jnp.where(left, turned, pltpu.roll(khigh[odd, :], 64, 1))
            buf[121:122, :] = jnp.where(left[:1], even_high[40:41], 0.0)
            lane = lax.broadcasted_iota(jnp.int32, (16, 128), 1)
            for m in range(8):
                start, skip = 15 * m + 24 * m // 128, 24 * m % 128
                tile = buf[start : start + 16, :]
                if skip:
                    tile = jnp.where(
                        lane < 128 - skip,
                        pltpu.roll(tile, 128 - skip, 1),
                        pltpu.roll(buf[start + 1 : start + 17, :], 128 - skip, 1),
                    )
                packed[m % 2, m // 2, quarter, where] = tile.astype(BF16)

    order = (1, 3, 2)
    other = 1 - core
    partner = device(y, z, x, other)
    pair_copies, x_copies, y_copies = {}, {}, {}

    def pair_stage(quarter):
        pair_copies[quarter].wait_recv()
        for r in order:
            xt = turn(x, r, 4)
            i = quarter * 3 + r - 1
            sx[r - 1, quarter] = total(packed[core, xt, quarter, 0:XZ], rc[quarter, xt, 0:XZ]).astype(BF16)
            x_copies[r, quarter] = send(
                sx.at[r - 1, quarter], rx.at[r - 1, quarter], x_send.at[i], x_recv.at[i], device(y, z, xt, core)
            )

    done = 0
    for quarter in range(4):
        until = (7, 14, 21, 27)[quarter]
        for tap in range(done, until):
            if tap not in local_taps:
                kernel_term(tap)
        done = until
        pack(quarter)
        pair_copies[quarter] = send(
            packed.at[other, :, quarter], rc.at[quarter], c_send.at[quarter], c_recv.at[quarter], partner
        )
        if quarter:
            pair_stage(quarter - 1)
    weights.wait()
    early = 4
    for tap in range(early):
        hidden_term(tap, tap == 0)
    pair_stage(3)
    for r in order:
        yt = turn(y, r, 4)
        sy[r - 1] = total(packed[core, :, yt, XZ:16], rc[yt, :, XZ:16]).astype(BF16)
        y_copies[r] = send(
            sy.at[r - 1], ry.at[r - 1], y_send.at[r - 1], y_recv.at[r - 1], device(turn(y, r, 4), z, x, core)
        )
    for tap in range(early, TAPS):
        hidden_term(tap)
    wide, inverse, normed, gate = norm()
    ngrad = acc[...] * gate * (1.0 + normed * (1.0 - gate))
    gain_sum = jnp.sum(ngrad * wide * inverse, axis=0, keepdims=True)
    g1[0:1, :] = gain_sum[:, :128]
    g1[1:2, :] = jnp.concatenate([gain_sum[:, 128:], jnp.zeros((1, 64), F32)], axis=1)
    gain_copies = [
        send(g1, q1.at[r - 1], q1_send.at[r - 1], q1_recv.at[r - 1], mate(r)) for r in range(1, 8)
    ]
    scaled = ngrad * gain[...]
    mean = jnp.mean(scaled * wide, axis=-1, keepdims=True)
    result = inverse * scaled - wide * (inverse * inverse * inverse) * mean
    vgrad[...] = result.astype(BF16).reshape(video.shape)

    def part_x(yt):
        return total(packed[core, x, yt, 0:XZ], rc[yt, x, 0:XZ], rx[0, yt], rx[1, yt], rx[2, yt])

    def part_y(xt):
        return total(packed[core, xt, y, XZ:16], rc[y, xt, XZ:16], ry[0, xt], ry[1, xt], ry[2, xt])

    second = {}
    for copy in x_copies.values():
        copy.wait_recv()
    for r in order:
        yt = turn(y, r, 4)
        sy2[r - 1] = part_x(yt).astype(BF16)
        second[r, 0] = send(
            sy2.at[r - 1], ry2.at[r - 1], b_send.at[r - 1], b_recv.at[r - 1], device(yt, z, x, core)
        )
    for copy in y_copies.values():
        copy.wait_recv()
    for r in order:
        xt = turn(x, r, 4)
        sx2[r - 1] = part_y(xt).astype(BF16)
        second[r, 1] = send(
            sx2.at[r - 1], rx2.at[r - 1], b_send.at[r + 2], b_recv.at[r + 2], device(y, z, xt, core)
        )
    for copy in gain_copies:
        copy.wait_recv()
    g2[...] = total(g1[...], *(q1[r] for r in range(7)))
    gain_second = [
        send(g2, q2.at[r - 1], q2_send.at[r - 1], q2_recv.at[r - 1], device(turn(y, r, 4), z, x, core))
        for r in range(1, 4)
    ]
    own_x, own_y = part_x(y), part_y(x)
    for copy in second.values():
        copy.wait_recv()
    s3[0:XZ] = total(own_x, ry2[0], ry2[1], ry2[2]).astype(BF16)
    s3[XZ:16] = total(own_y, rx2[0], rx2[1], rx2[2]).astype(BF16)
    pl.semaphore_wait(far_sem, 2)
    third, gain_third = [], []
    hops = (8, 7, 9, 6, 10, 5, 11, 4, 12, 3, 13, 2, 14, 1, 15)
    for r in hops:
        zt = turn(z, r, 16)
        third.append(
            send(s3.at[zt], r3.at[r - 1], z_send.at[r - 1], z_recv.at[r - 1], device(y, zt, x, core))
        )
    for copy in gain_second:
        copy.wait_recv()
    g3[...] = total(g2[...], *(q2[r] for r in range(3)))
    for r in hops:
        gain_third.append(
            send(g3, q3.at[r - 1], q3_send.at[r - 1], q3_recv.at[r - 1], device(y, turn(z, r, 16), x, core))
        )
    for copy in third:
        copy.wait_recv()
    final = total(s3[z], *(r3[r] for r in range(15))) * (1.0 / 512)
    out[...] = final
    for copy in gain_third:
        copy.wait_recv()
    gain_out[...] = total(g3[...], *(q3[r] for r in range(15))) * (1.0 / 512)
    for group in (
        halo, pair_copies.values(), x_copies.values(), y_copies.values(), gain_copies,
        second.values(), gain_second, third, gain_third,
    ):
        for copy in group:
            copy.wait_send()


def fused(video, gain, kernel, cot):
    frames, rows, cols, _ = video.shape
    pixels = frames * rows * cols
    vmem = pl.BlockSpec(memory_space=pltpu.VMEM)

    def tiles(*shape):
        return pltpu.VMEM(shape + (16, 128), BF16)

    def line(*shape):
        return pltpu.VMEM(shape + (2, 128), F32)

    def dma(count):
        return [pltpu.SemaphoreType.DMA((count,))] * 2

    return pl.pallas_call(
        fused_kernel,
        out_shape=(
            pltpu.VMEM(video.shape, BF16),
            pltpu.VMEM((16, 128), F32),
            pltpu.VMEM((2, 128), F32),
        ),
        in_specs=[pl.BlockSpec(memory_space=pl.ANY)] * 4,
        out_specs=(vmem, vmem, vmem),
        scratch_shapes=[
            pltpu.VMEM(video.shape, BF16),
            pltpu.VMEM((1, C), F32),
            pltpu.VMEM(cot.shape, BF16),
            pltpu.VMEM((TAPS, C, C), BF16),
            pltpu.VMEM((frames + 2, rows + 2, cols, C), BF16),
            pltpu.VMEM((3, frames + 2, rows + 2, cols, C), BF16),
            pltpu.VMEM((C, pixels), BF16),
            pltpu.VMEM((TAPS * C, 128), F32),
            pltpu.VMEM((TAPS * C, 128), F32),
            pltpu.VMEM((4, 128, 128), F32),
            pltpu.VMEM((pixels, C), F32),
            tiles(2, 4, 4, 16),
            tiles(4, 4, 16),
            tiles(3, 4, XZ), tiles(3, 4, XZ), tiles(3, 4, 16 - XZ), tiles(3, 4, 16 - XZ),
            tiles(3, 16 - XZ), tiles(3, 16 - XZ), tiles(3, XZ), tiles(3, XZ),
            tiles(16), tiles(15),
            line(), line(7), line(), line(3), line(), line(15),
            *[pltpu.SemaphoreType.DMA] * 4, pltpu.SemaphoreType.REGULAR,
            *dma(5), *dma(4), *dma(12), *dma(3), *dma(6), *dma(15),
            *dma(7), *dma(3), *dma(15),
        ],
        compiler_params=pltpu.CompilerParams(
            collective_id=0, has_side_effects=True, vmem_limit_bytes=59 << 20
        ),
        name="fused_backward",
    )(video, gain.reshape(1, C), kernel.reshape(TAPS, C, C), cot)


def finish_kernel(vgrad, tile, gain_rows, vgrad_out, share, gain_out):
    vgrad_out[...] = vgrad[...]
    gain_out[0:128] = gain_rows[0]
    gain_out[128:C] = gain_rows[1, : C - 128]
    for a in range(15):
        share[128 * a : 128 * a + 128] = tile[a]
    share[1920:1944] = tile[15, :24]


def finish(vgrad, tile, gain_rows):
    vmem = pl.BlockSpec(memory_space=pltpu.VMEM)
    return pl.pallas_call(
        finish_kernel,
        out_shape=(
            jax.ShapeDtypeStruct(vgrad.shape, BF16),
            jax.ShapeDtypeStruct((1944,), F32),
            jax.ShapeDtypeStruct((C,), F32),
        ),
        in_specs=[vmem] * 3,
        out_specs=(vmem,) * 3,
        compiler_params=pltpu.CompilerParams(vmem_limit_bytes=8 << 20),
        name="finish",
    )(vgrad, tile, gain_rows)


def on_device(video, gain, kernel, cotangent):
    return finish(*fused(video, gain, kernel, cotangent))


def solution(mesh):
    in_specs = (P("tm", "space", None, None), P(), P(), P("tm", "space", None, None))
    out_specs = (P("tm", "space", None, None), P(("tm", "space")), P())
    return jax.shard_map(
        on_device, mesh=mesh, in_specs=in_specs, out_specs=out_specs, check_vma=False
    )
```
